32 devices in a mesh: row: 8 (over y, x, core), col: 4 (over z).
Axes of the slice: x: 2, y: 2, z: 4, core: 2. Of those that a mesh axis runs over, the one named last changes fastest.
Arguments:
- tiles: bfloat16 [8, 64, 128, 128], P('row', 'col'), may hold values from -2 to 2
- tile_index: int32 [8, 64], P('row', 'col'), may hold values from 0 to 16384, as said below
- u_basis: float32 [64, 131072], P(None, ('row', 'col')), may hold values from -10 to 10
- v_basis: float32 [64, 4, 16384], P(None, 'col', 'row'), may hold values from -10 to 10
- v_start: float32 [65536], P('col'), may hold values from -0.5 to 1.5
Outputs:
- left_vectors: float32 [2, 131072], P(None, ('row', 'col'))
- right_vectors: float32 [2, 4, 16384], P(None, 'col', 'row')
- bidiagonal: float32 [2, 2], replicated
The draws below stay inside these ranges and needn't reach their ends.
Inputs may be any that keep to these rules, and one draw needn't show every extreme that they name: `tile_index`: each block's 16 slots name distinct tiles of its 128 x 128 block as r * 128 + c; the value 128 * 128 marks an empty slot, and empty slots come after all live ones. Blocks have different numbers of live slots, at least 4; some block has all 16 slots live.
All inputs are finite; a program needn't handle non-finite values.
Results may differ from the reference program's by a relative error of at most 0.0003.
Values sent between devices are 32-bit elements; how exact they have to be, the bound alone decides.
No kernel may reach another device: no remote copies, remote signals or barrier semaphores. Data moves between devices by JAX's collectives and lax.ppermute only.
A program may use at most 64 MiB of HBM per device.

```python
import math
import jax
import jax.numpy as jnp
from jax import lax

TB = 128
KB = 64
ITERS = 2
BR = 128
BC = 128
NT = 16
NROWS = 131072
NCOLS = 65536
N_ROW = 8
N_COL = 4


def draw_tiles(key, part):
    key = jax.random.fold_in(key, 3)
    first_key, second_key = jax.random.split(key)
    shape = (N_ROW, N_COL * NT, TB, TB)
    noise = jnp.clip(jax.random.normal(first_key, shape, jnp.float32), -6.0, 6.0)
    spread = jnp.exp(jax.random.uniform(second_key, (N_ROW, N_COL * NT, 1, 1), jnp.float32, -0.6931472, 0.6931472))
    rising = 1.0 + 2.0 * jnp.arange(N_ROW, dtype=jnp.float32) / max(N_ROW - 1, 1)
    factor = 0.5 / math.sqrt(N_COL * NT * TB / BR)
    result = (noise + 0.03) * spread * rising[:, None, None, None] * factor
    return jnp.clip(result, -2.0, 2.0).astype(jnp.bfloat16)


def draw_tile_index(key, part):
    key = jax.random.fold_in(key, 4)
    devices = N_ROW * N_COL
    device_keys = jax.random.split(key, devices)

    def one_device(device_key):
        order_key, count_key = jax.random.split(device_key)
        order = jax.random.permutation(order_key, BR * BC)[:NT].astype(jnp.int32)
        count = jax.random.randint(count_key, (), max(1, NT // 4), NT + 1)
        live = jnp.where(jnp.arange(NT) < count, order, BR * BC)
        return (order, live)
    orders, lives = jax.vmap(one_device)(device_keys)
    chosen = jax.random.randint(jax.random.fold_in(key, 9), (), 0, devices)
    table = jnp.where((jnp.arange(devices) == chosen)[:, None], orders, lives)
    return table.reshape(N_ROW, N_COL * NT).astype(jnp.int32)


def draw_basis(key, count, extent):
    noise_key, mix_key, mean_key = jax.random.split(key, 3)
    noise = jnp.clip(jax.random.normal(noise_key, (count, extent), jnp.float32), -6.0, 6.0)
    mixing = jax.random.normal(mix_key, (count, count), jnp.float32) * (0.15 / math.sqrt(count))
    offsets = jax.random.normal(mean_key, (count, 1), jnp.float32) * 0.07
    result = noise + jnp.dot(mixing, noise, precision=lax.Precision.HIGHEST) + offsets
    return jnp.clip(result, -10.0, 10.0)


def draw_u_basis(key, part):
    return draw_basis(jax.random.fold_in(key, 1), KB, NROWS)


def draw_v_basis(key, part):
    return draw_basis(jax.random.fold_in(key, 2), KB, NCOLS).reshape(KB, N_COL, BC * TB)


def levels(stream_key, dims, cuts, smallest, high):
    gain = 1.0
    for axis_at, shards_of in cuts:
        steps = jax.random.uniform(jax.random.fold_in(jax.random.fold_in(stream_key, 6), axis_at), (shards_of,), jnp.float32, smallest / len(cuts), high / len(cuts))
        gain = gain * jnp.repeat(jnp.exp(steps), dims[axis_at] // shards_of).reshape((-1,) + (1,) * (len(dims) - 1 - axis_at))
    return gain


def setup_inputs(seed: int = 0) -> dict:
    key_list = jax.random.split(jax.random.key(seed), 6)
    tiles = draw_tiles(jax.random.fold_in(key_list[5], 71), 0)
    tile_index = draw_tile_index(jax.random.fold_in(key_list[5], 71), 0)
    u_basis = draw_u_basis(jax.random.fold_in(key_list[5], 71), 0)
    v_basis = draw_v_basis(jax.random.fold_in(key_list[5], 71), 0)
    v_start = jnp.clip(-0.5 + 2.0 * jax.random.uniform(key_list[4], (NCOLS,), jnp.float32) ** levels(key_list[4], (NCOLS,), ((0, 4),), -0.2, 0.2), -0.5, 1.5)
    return dict(tiles=tiles, tile_index=tile_index, u_basis=u_basis, v_basis=v_basis, v_start=v_start)


HIGHEST = lax.Precision.HIGHEST
EPSILON = 1e-06

def masks(slots):
    rows_hot = (slots[..., None] // BC == jnp.arange(BR)).astype(jnp.float32)
    cols_hot = (slots[..., None] % BC == jnp.arange(BC)).astype(jnp.float32)
    return (rows_hot, cols_hot)

def forward(tiles, tile_index, vector):
    blocks = tiles.reshape(N_ROW, N_COL, NT, TB, TB)
    slots = tile_index.reshape(N_ROW, N_COL, NT)
    pieces = vector.reshape(N_COL, BC, TB)

    def one_row(entry):
        block, slot = entry
        rows_hot, cols_hot = masks(slot)
        picked = jnp.einsum('jtc,jck->jtk', cols_hot, pieces, precision=HIGHEST)
        product = jnp.einsum('jtab,jtb->jta', block.astype(jnp.float32), picked, precision=HIGHEST)
        return jnp.einsum('jtr,jta->ra', rows_hot, product, precision=HIGHEST)
    return lax.map(one_row, (blocks, slots)).reshape(NROWS)

def backward(tiles, tile_index, vector):
    blocks = tiles.reshape(N_ROW, N_COL, NT, TB, TB)
    slots = tile_index.reshape(N_ROW, N_COL, NT)
    pieces = vector.reshape(N_ROW, BR, TB)

    def one_row(total, entry):
        block, slot, piece = entry
        rows_hot, cols_hot = masks(slot)
        picked = jnp.einsum('jtr,rk->jtk', rows_hot, piece, precision=HIGHEST)
        product = jnp.einsum('jtab,jta->jtb', block.astype(jnp.float32), picked, precision=HIGHEST)
        return (total + jnp.einsum('jtc,jtb->jcb', cols_hot, product, precision=HIGHEST), None)
    total, _ = lax.scan(one_row, jnp.zeros((N_COL, BC, TB), jnp.float32), (blocks, slots, pieces))
    return total.reshape(NCOLS)

def reorthogonalize(vector, basis, length):
    first = jnp.dot(basis, vector, precision=HIGHEST) / length
    once = vector - jnp.dot(first, basis, precision=HIGHEST)
    second = jnp.dot(basis, once, precision=HIGHEST) / length
    twice = once - jnp.dot(second, basis, precision=HIGHEST)
    scale = jnp.sqrt(jnp.sum(twice * twice) / length + EPSILON)
    return (twice / scale, scale)

def reference(tiles, tile_index, u_basis, v_basis, v_start):
    left_basis = u_basis
    right_basis = jnp.concatenate([v_basis.reshape(KB, NCOLS), v_start[None, :]], 0)
    vector = v_start
    lefts, rights, alphas, betas = ([], [], [], [])
    for iteration in range(ITERS):
        image = forward(tiles, tile_index, vector)
        left_unit, alpha = reorthogonalize(image, left_basis, NROWS)
        left_basis = jnp.concatenate([left_basis, left_unit[None, :]], 0)
        back_image = backward(tiles, tile_index, left_unit)
        vector, beta = reorthogonalize(back_image, right_basis, NCOLS)
        right_basis = jnp.concatenate([right_basis, vector[None, :]], 0)
        lefts.append(left_unit)
        rights.append(vector)
        alphas.append(alpha)
        betas.append(beta)
    left_vectors = jnp.stack(lefts)
    right_vectors = jnp.stack(rights).reshape(ITERS, N_COL, BC * TB)
    bidiagonal = jnp.stack([jnp.stack(alphas), jnp.stack(betas)])
    return (left_vectors, right_vectors, bidiagonal)
```

```python
import jax
import jax.numpy as jnp
from jax import lax
from jax.sharding import PartitionSpec as P

ITERS = 2


HIGHEST = lax.Precision.HIGHEST
EPSILON = 1e-06
BOTH = ("row", "col")


def swap(chunks, axis):
    return lax.all_to_all(chunks, axis, 0, 0, tiled=True)


def reduce_scatter(chunks, axis):
    return jnp.sum(swap(chunks, axis), 0)


def gather(piece, axis):
    count = lax.axis_size(axis)
    return swap(jnp.broadcast_to(piece[None], (count,) + piece.shape), axis)


def project_gram(share, basis, gram, coeffs, squares, total):
    coeffs = coeffs / total
    squares = squares / total
    second = coeffs - jnp.dot(gram, coeffs, precision=HIGHEST)
    combined = coeffs + second
    gram_comb = jnp.dot(gram, combined, precision=HIGHEST)
    remaining = coeffs - gram_comb
    squared = (
        squares
        - 2.0 * jnp.dot(combined, coeffs, precision=HIGHEST)
        + jnp.dot(combined, gram_comb, precision=HIGHEST)
    )
    scale = jnp.sqrt(squared + EPSILON)
    unit = (share - jnp.dot(combined, basis, precision=HIGHEST)) / scale
    column = remaining / scale
    corner = squared / (scale * scale)
    upper = jnp.concatenate([gram, column[:, None]], 1)
    lower = jnp.concatenate([column, corner[None]])[None, :]
    return (unit, scale, jnp.concatenate([upper, lower], 0))


def shards(tiles, tile_index, u_basis, v_basis, v_start):
    blocks = tiles[0].astype(jnp.float32)
    slots = tile_index[0]
    width = blocks.shape[1]
    cols_len = v_start.shape[0]
    col_blocks = cols_len // width
    row_count = lax.axis_size("row")
    col_count = lax.axis_size("col")
    devices = row_count * col_count
    left_piece = u_basis.shape[1]
    right_piece = v_basis.shape[2]
    rows_len = left_piece * col_count
    row_blocks = rows_len // width
    total_left = rows_len * row_count
    total_right = cols_len * col_count
    rows_hot = (slots[:, None] // col_blocks == jnp.arange(row_blocks)[None, :]).astype(jnp.float32)
    cols_hot = (slots[:, None] % col_blocks == jnp.arange(col_blocks)[None, :]).astype(jnp.float32)
    right_start = lax.axis_index("row") * right_piece

    def forward(vector):
        picked = jnp.dot(cols_hot, vector.reshape(col_blocks, width), precision=HIGHEST)
        product = jnp.einsum("tab,tb->ta", blocks, picked, precision=HIGHEST)
        dense = jnp.einsum("tr,ta->ra", rows_hot, product, precision=HIGHEST)
        return reduce_scatter(dense.reshape(col_count, left_piece), "col")

    def backward(vector):
        picked = jnp.dot(rows_hot, vector.reshape(row_blocks, width), precision=HIGHEST)
        product = jnp.einsum("tab,ta->tb", blocks, picked, precision=HIGHEST)
        dense = jnp.einsum("tc,tb->cb", cols_hot, product, precision=HIGHEST)
        return reduce_scatter(dense.reshape(row_count, right_piece), "row")

    left_basis = u_basis
    start_share = lax.dynamic_slice_in_dim(v_start, right_start, right_piece)
    right_basis = jnp.concatenate([v_basis[:, 0, :], start_share[None, :]], 0)
    kept = left_basis.shape[0]
    kept_right = right_basis.shape[0]
    grams = jnp.concatenate(
        [
            jnp.dot(left_basis, left_basis.T, precision=HIGHEST).reshape(-1),
            jnp.dot(right_basis, right_basis.T, precision=HIGHEST).reshape(-1),
        ]
    )
    gram_len = grams.shape[0]
    chunk = -(-gram_len // devices)
    grams = jnp.pad(grams, (0, chunk * devices - gram_len)).reshape(devices, chunk)
    gram_chunk = reduce_scatter(grams, BOTH)
    vector = v_start
    lefts, rights, alphas, betas = ([], [], [], [])
    for iteration in range(ITERS):
        share = forward(vector)
        sent = [jnp.dot(left_basis, share, precision=HIGHEST), jnp.sum(share * share)[None]]
        size = left_basis.shape[0]
        if iteration == 0:
            sent.append(gram_chunk)
        received = gather(jnp.concatenate(sent), BOTH)
        summed = jnp.sum(received[:, : size + 1], 0)
        if iteration == 0:
            whole = received[:, size + 1 :].reshape(-1)
            left_gram = whole[: kept * kept].reshape(kept, kept) / total_left
            right_gram = whole[kept * kept : gram_len].reshape(kept_right, kept_right) / total_right
        left_unit, alpha, left_gram = project_gram(
            share, left_basis, left_gram, summed[:size], summed[size], total_left
        )
        left_basis = jnp.concatenate([left_basis, left_unit[None, :]], 0)
        share = backward(gather(left_unit, "col").reshape(-1))
        size = right_basis.shape[0]
        sent = [jnp.dot(right_basis, share, precision=HIGHEST), jnp.sum(share * share)[None]]
        summed = jnp.sum(gather(jnp.concatenate(sent), BOTH), 0)
        right_unit, beta, right_gram = project_gram(
            share, right_basis, right_gram, summed[:size], summed[size], total_right
        )
        right_basis = jnp.concatenate([right_basis, right_unit[None, :]], 0)
        if iteration + 1 < ITERS:
            vector = gather(right_unit, "row").reshape(-1)
        lefts.append(left_unit)
        rights.append(right_unit)
        alphas.append(alpha)
        betas.append(beta)
    left_vectors = jnp.stack(lefts)
    right_vectors = jnp.stack(rights)[:, None, :]
    bidiagonal = jnp.stack([jnp.stack(alphas), jnp.stack(betas)])
    return (left_vectors, right_vectors, bidiagonal)


def solution(mesh):
    placed = (
        P("row", "col", None, None),
        P("row", "col"),
        P(None, ("row", "col")),
        P(None, "col", "row"),
        P("col"),
    )
    return jax.shard_map(
        shards,
        mesh=mesh,
        in_specs=placed,
        out_specs=(P(None, ("row", "col")), P(None, "col", "row"), P()),
        check_vma=False,
    )
```

```python
import jax
import jax.numpy as jnp
from jax import lax
from jax.experimental import pallas as pl
from jax.experimental.pallas import tpu as pltpu
from jax.sharding import PartitionSpec as P

ITERS = 2


HIGHEST = lax.Precision.HIGHEST
EPSILON = 1e-06
BOTH = ("row", "col")
LANES = 128
GROUP = 8
PARAMS = pltpu.CompilerParams(vmem_limit_bytes=8 * 2**20)
VMEM = pl.BlockSpec(memory_space=pltpu.VMEM)
SMEM = pl.BlockSpec(memory_space=pltpu.SMEM)


def swap(chunks, axis):
    return lax.all_to_all(chunks, axis, 0, 0, tiled=True)


def call(kernel, outs, args, specs=None):
    shapes = tuple(jax.ShapeDtypeStruct(shape, jnp.float32) for shape in outs)
    return pl.pallas_call(
        kernel,
        out_shape=shapes,
        in_specs=specs or [VMEM] * len(args),
        out_specs=tuple([VMEM] * len(outs)),
        compiler_params=PARAMS,
    )(*args)


def three_parts(x):
    high = x.astype(jnp.bfloat16)
    rest = x - high.astype(jnp.float32)
    middle = rest.astype(jnp.bfloat16)
    low = (rest - middle.astype(jnp.float32)).astype(jnp.bfloat16)
    return jnp.concatenate([high, middle, low], 0)


def multiply_tiles(tiles, slots, vector, in_blocks, out_blocks, is_forward):
    count, width = tiles.shape[0], tiles.shape[1]
    divisor = in_blocks if is_forward else out_blocks
    limit = in_blocks * out_blocks

    def kernel(slots_ref, tiles_ref, vector_ref, dense_ref, picked_ref):
        dense_ref[...] = jnp.zeros_like(dense_ref)
        for t in range(count):
            slot = jnp.minimum(slots_ref[t], limit - 1)
            row = slot // divisor
            source = slot - row * divisor if is_forward else row
            picked_ref[pl.ds(t, 1), :] = vector_ref[pl.ds(source, 1), :]
        parts = three_parts(picked_ref[...])
        contract = (((1,), (1,)), ((), ())) if is_forward else (((1,), (0,)), ((), ()))
        for t in range(count):
            result = lax.dot_general(parts, tiles_ref[t], contract, preferred_element_type=jnp.float32)
            slot = slots_ref[t]
            live = slot < limit
            slot = jnp.minimum(slot, limit - 1)
            row = slot // divisor
            target = row if is_forward else slot - row * divisor
            value = (
                result[t : t + 1]
                + result[count + t : count + t + 1]
                + result[2 * count + t : 2 * count + t + 1]
            )
            value = jnp.where(live, value, 0.0)
            dense_ref[pl.ds(target, 1), :] = dense_ref[pl.ds(target, 1), :] + value

    return pl.pallas_call(
        kernel,
        out_shape=jax.ShapeDtypeStruct((out_blocks, width), jnp.float32),
        in_specs=[SMEM, VMEM, VMEM],
        out_specs=VMEM,
        scratch_shapes=[pltpu.VMEM((count, width), jnp.float32)],
        compiler_params=PARAMS,
    )(slots, tiles, vector)


def diagonal(rows):
    shape = (rows, LANES)
    return lax.broadcasted_iota(jnp.int32, shape, 0) == lax.broadcasted_iota(jnp.int32, shape, 1)


def as_row(column):
    return jnp.sum(jnp.where(diagonal(column.shape[0]), column, 0.0), 0, keepdims=True)


def total_sum(x):
    return jnp.sum(jnp.sum(x, 0, keepdims=True), 1, keepdims=True)


def inner_products(received, basis, extras, copies):
    kept = basis.shape[0]
    rows = received.shape[1]

    def kernel(received_ref, basis_ref, *refs):
        extra_refs, piece_ref, row_ref = refs[: len(extras)], refs[-2], refs[-1]
        piece = jnp.sum(received_ref[...], 0)
        piece_ref[...] = piece
        total = jnp.zeros((kept, LANES), jnp.float32)
        for k in range(rows):
            total = total + basis_ref[:, k * LANES : (k + 1) * LANES] * piece[k : k + 1, :]
        row = as_row(jnp.sum(total, 1, keepdims=True))
        lane = lax.broadcasted_iota(jnp.int32, (1, LANES), 1)
        for e, extra_ref in enumerate(extra_refs):
            row = row + jnp.where(lane == kept + e, total_sum(extra_ref[...] * piece), 0.0)
        row = row + jnp.where(lane == LANES - 1, total_sum(piece * piece), 0.0)
        row_ref[...] = jnp.broadcast_to(row, row_ref.shape)

    return call(kernel, [(rows, LANES), (copies, LANES)], [received, basis, *extras])


def new_vector(rows_received, gram, piece, basis, extras, total, copies):
    kept = basis.shape[0]
    rows = piece.shape[0]
    size = kept + len(extras)
    padded = gram.shape[0]

    def kernel(received_ref, gram_ref, piece_ref, basis_ref, *refs):
        extra_refs = refs[: len(extras)]
        copies_ref, gram_out_ref, scale_ref = refs[len(extras) :]
        sums = jnp.sum(received_ref[...], 0, keepdims=True) * (1.0 / total)
        lane = lax.broadcasted_iota(jnp.int32, (1, LANES), 1)
        coeffs = jnp.where(lane < size, sums, 0.0)
        squares = jnp.sum(jnp.where(lane == LANES - 1, sums, 0.0), 1, keepdims=True)
        products = gram_ref[...]
        eye = diagonal(padded)
        coeffs_col = jnp.sum(jnp.where(eye, coeffs, 0.0), 1, keepdims=True)
        combined = 2.0 * coeffs_col - jnp.sum(products * coeffs, 1, keepdims=True)
        gram_comb = jnp.sum(products * as_row(combined), 1, keepdims=True)
        remaining = coeffs_col - gram_comb
        squared = squares + jnp.sum(combined * (gram_comb - 2.0 * coeffs_col), 0, keepdims=True)
        squared = jnp.maximum(squared, 0.0)
        scale = jnp.sqrt(squared + EPSILON)
        inverse = 1.0 / scale
        spread = jnp.broadcast_to(combined[:kept], (kept, LANES))
        own = piece_ref[...]
        for e, extra_ref in enumerate(extra_refs):
            own = own - combined[kept + e : kept + e + 1] * extra_ref[...]
        for k in range(rows):
            part = jnp.sum(spread * basis_ref[:, k * LANES : (k + 1) * LANES], 0, keepdims=True)
            line = (own[k : k + 1, :] - part) * inverse
            for copy in range(copies):
                copies_ref[copy, pl.ds(k, 1), :] = line
        remaining = remaining * inverse
        sub_at = lax.broadcasted_iota(jnp.int32, (padded, LANES), 0)
        lane_at = lax.broadcasted_iota(jnp.int32, (padded, LANES), 1)
        wider = jnp.where((lane_at == size) & (sub_at < size), remaining, products)
        wider = jnp.where((sub_at == size) & (lane_at < size), as_row(remaining), wider)
        wider = jnp.where((sub_at == size) & (lane_at == size), squared * inverse * inverse, wider)
        gram_out_ref[...] = wider
        scale_ref[...] = jnp.broadcast_to(scale, scale_ref.shape)

    return call(
        kernel,
        [(copies, rows, LANES), (padded, LANES), (1, LANES)],
        [rows_received, gram, piece, basis, *extras],
    )


def shards(tiles, tile_index, u_basis, v_basis, v_start):
    blocks = tiles[0]
    slots = tile_index[0]
    width = blocks.shape[1]
    cols_len = v_start.shape[0]
    col_blocks = cols_len // width
    row_count = lax.axis_size("row")
    col_count = lax.axis_size("col")
    devices = row_count * col_count
    kept = u_basis.shape[0]
    left_piece = u_basis.shape[1]
    right_piece = v_basis.shape[2]
    rows_len = left_piece * col_count
    row_blocks = rows_len // width
    left_rows = left_piece // width
    right_rows = right_piece // width
    total_left = rows_len * row_count
    total_right = cols_len * col_count
    padded = kept + GROUP

    whole_start = v_start.reshape(col_blocks, width)
    dense = multiply_tiles(blocks, slots, whole_start, col_blocks, row_blocks, True)
    chunks = dense.reshape(col_count, left_rows, width)
    me = lax.axis_index("col")
    arrived = [lax.dynamic_index_in_dim(chunks, me, 0, True)]
    for shift in range(1, col_count):
        pairs = [(i, (i + shift) % col_count) for i in range(col_count)]
        chunk = lax.dynamic_index_in_dim(chunks, (me + shift) % col_count, 0, True)
        arrived.append(lax.ppermute(chunk, "col", pairs))
    received = jnp.concatenate(arrived, 0)

    right_basis = v_basis[:, 0, :]
    start_share = lax.dynamic_slice_in_dim(
        whole_start, lax.axis_index("row") * right_rows, right_rows, 0
    )
    grams = jnp.concatenate(
        [
            jnp.dot(u_basis, u_basis.T, precision=HIGHEST) / total_left,
            jnp.dot(right_basis, right_basis.T, precision=HIGHEST) / total_right,
        ],
        1,
    )
    chunk = grams.size // devices
    gram_chunk = jnp.sum(swap(grams.reshape(devices, chunk), BOTH), 0)
    chunk_rows = -(-chunk // LANES)
    gram_chunk = jnp.pad(gram_chunk, (0, chunk_rows * LANES - chunk)).reshape(1, chunk_rows, LANES)
    _, start_row = inner_products(start_share[None], right_basis, [start_share], 1)

    lefts, rights, alphas, betas = ([], [], [], [])
    left_extras, right_extras = ([], [start_share])
    for iteration in range(ITERS):
        piece, row = inner_products(received, u_basis, left_extras, devices)
        row = row.reshape(devices, 1, LANES)
        if iteration == 0:
            start_rows = jnp.broadcast_to(start_row[None], (devices, 1, LANES))
            chunk_sent = jnp.broadcast_to(gram_chunk, (devices, chunk_rows, LANES))
            everything = swap(jnp.concatenate([row, start_rows, chunk_sent], 1), BOTH)
            summed_rows = everything[:, 0, :]
            start_products = jnp.sum(everything[:, 1, :], 0) / total_right
            whole = everything[:, 2:, :].reshape(devices, chunk_rows * LANES)[:, :chunk]
            whole = whole.reshape(kept, 2 * kept)
            left_gram = jnp.pad(whole[:, :kept], ((0, GROUP), (0, LANES - kept)))
            lane = jnp.arange(LANES)
            start_products = jnp.where(lane <= kept, start_products, 0.0)
            right_gram = jnp.pad(whole[:, kept:], ((0, GROUP), (0, LANES - kept)))
            right_gram = right_gram.at[kept, :].set(start_products)
            right_gram = right_gram.at[:, kept].set(start_products[:padded])
        else:
            summed_rows = swap(row, BOTH).reshape(devices, LANES)
        copies, left_gram, alpha = new_vector(
            summed_rows, left_gram, piece, u_basis, left_extras, total_left, col_count
        )
        left_unit = copies[0]
        left_extras = left_extras + [left_unit]
        joined = swap(copies, "col").reshape(row_blocks, width)
        dense = multiply_tiles(blocks, slots, joined, row_blocks, col_blocks, False)
        received = swap(dense.reshape(row_count, right_rows, width), "row")
        piece, row = inner_products(received, right_basis, right_extras, devices)
        summed_rows = swap(row.reshape(devices, 1, LANES), BOTH).reshape(devices, LANES)
        copies, right_gram, beta = new_vector(
            summed_rows, right_gram, piece, right_basis, right_extras, total_right, row_count
        )
        right_unit = copies[0]
        right_extras = right_extras + [right_unit]
        if iteration + 1 < ITERS:
            joined = swap(copies, "row").reshape(col_blocks, width)
            dense = multiply_tiles(blocks, slots, joined, col_blocks, row_blocks, True)
            received = swap(dense.reshape(col_count, left_rows, width), "col")
        lefts.append(left_unit.reshape(-1))
        rights.append(right_unit.reshape(-1))
        alphas.append(alpha[0, 0])
        betas.append(beta[0, 0])
    left_vectors = jnp.stack(lefts)
    right_vectors = jnp.stack(rights)[:, None, :]
    bidiagonal = jnp.stack([jnp.stack(alphas), jnp.stack(betas)])
    return (left_vectors, right_vectors, bidiagonal)


def solution(mesh):
    placed = (
        P("row", "col", None, None),
        P("row", "col"),
        P(None, ("row", "col")),
        P(None, "col", "row"),
        P("col"),
    )
    return jax.shard_map(
        shards,
        mesh=mesh,
        in_specs=placed,
        out_specs=(P(None, ("row", "col")), P(None, "col", "row"), P()),
        check_vma=False,
    )
```

```python
import jax
import jax.numpy as jnp
from jax import lax
from jax.experimental import pallas as pl
from jax.experimental.pallas import tpu as pltpu
from jax.sharding import PartitionSpec as P

ITERS = 2


HIGHEST = lax.Precision.HIGHEST
EPSILON = 1e-06
BOTH = ("row", "col")
LANES = 128
GROUP = 8
PARAMS = pltpu.CompilerParams(vmem_limit_bytes=8 * 2**20)
VMEM = pl.BlockSpec(memory_space=pltpu.VMEM)
SMEM = pl.BlockSpec(memory_space=pltpu.SMEM)


def swap(chunks, axis):
    return lax.all_to_all(chunks, axis, 0, 0, tiled=True)


def call(kernel, outs, args, specs=None):
    shapes = tuple(jax.ShapeDtypeStruct(shape, jnp.float32) for shape in outs)
    return pl.pallas_call(
        kernel,
        out_shape=shapes,
        in_specs=specs or [VMEM] * len(args),
        out_specs=tuple([VMEM] * len(outs)),
        compiler_params=PARAMS,
    )(*args)


def three_parts(x):
    high = x.astype(jnp.bfloat16)
    rest = x - high.astype(jnp.float32)
    middle = rest.astype(jnp.bfloat16)
    low = (rest - middle.astype(jnp.float32)).astype(jnp.bfloat16)
    return jnp.concatenate([high, middle, low], 0)


def multiply_tiles(tiles, slots, vector, in_blocks, out_blocks, is_forward):
    count, width = tiles.shape[0], tiles.shape[1]
    divisor = in_blocks if is_forward else out_blocks
    limit = in_blocks * out_blocks
    contract = (((1,), (1,)), ((), ())) if is_forward else (((1,), (0,)), ((), ()))

    def kernel(slots_ref, tiles_ref, vector_ref, dense_ref, picked_ref, product_ref):
        targets = []
        for t in range(count):
            slot = slots_ref[t]
            live = slot < limit
            slot = jnp.where(live, slot, 0)
            row = lax.div(slot, divisor)
            column = slot - row * divisor
            source = column if is_forward else row
            targets.append(row if is_forward else column)
            line = vector_ref[pl.ds(source, 1), :]
            picked_ref[pl.ds(t, 1), :] = jnp.where(live, line, 0.0)
        parts = three_parts(picked_ref[...])
        dense_ref[...] = jnp.zeros_like(dense_ref)
        for t in range(count):
            result = lax.dot_general(parts, tiles_ref[t], contract, preferred_element_type=jnp.float32)
            product_ref[pl.ds(t, 1), :] = (
                result[t : t + 1]
                + result[count + t : count + t + 1]
                + result[2 * count + t : 2 * count + t + 1]
            )
        for t in range(count):
            line = pl.ds(targets[t], 1)
            dense_ref[line, :] = dense_ref[line, :] + product_ref[pl.ds(t, 1), :]

    return pl.pallas_call(
        kernel,
        out_shape=jax.ShapeDtypeStruct((out_blocks, width), jnp.float32),
        in_specs=[SMEM, VMEM, VMEM],
        out_specs=VMEM,
        scratch_shapes=[pltpu.VMEM((count, width), jnp.float32)] * 2,
        compiler_params=PARAMS,
    )(slots, tiles, vector)


def diagonal(rows):
    shape = (rows, LANES)
    return lax.broadcasted_iota(jnp.int32, shape, 0) == lax.broadcasted_iota(jnp.int32, shape, 1)


def as_row(column):
    return jnp.sum(jnp.where(diagonal(column.shape[0]), column, 0.0), 0, keepdims=True)


def total_sum(x):
    return jnp.sum(jnp.sum(x, 0, keepdims=True), 1, keepdims=True)


def basis_products(piece, basis_ref, extra_pieces):
    kept = basis_ref.shape[0]
    total = jnp.zeros((kept, LANES), jnp.float32)
    for k in range(piece.shape[0]):
        total = total + basis_ref[:, k * LANES : (k + 1) * LANES] * piece[k : k + 1, :]
    row = as_row(jnp.sum(total, 1, keepdims=True))
    lane = lax.broadcasted_iota(jnp.int32, (1, LANES), 1)
    for e, extra in enumerate(extra_pieces):
        row = row + jnp.where(lane == kept + e, total_sum(extra * piece), 0.0)
    return row + jnp.where(lane == LANES - 1, total_sum(piece * piece), 0.0)


def first_grams(u_basis, right_basis, start_share, after, total_left, total_right):
    kept = u_basis.shape[0]
    contract = (((1,), (1,)), ((), ()))

    def kernel(u_ref, v_ref, start_ref, after_ref, grams_ref, row_ref):
        for at, ref, total in ((0, u_ref, total_left), (kept, v_ref, total_right)):
            basis = ref[...]
            gram = lax.dot_general(
                basis, basis, contract, precision=HIGHEST, preferred_element_type=jnp.float32
            )
            grams_ref[:, at : at + kept] = gram * (1.0 / total)
        start = start_ref[...]
        row_ref[...] = basis_products(start, v_ref, [start])

    return call(
        kernel, [(kept, 2 * kept), (1, LANES)], [u_basis, right_basis, start_share, after]
    )


def first_products(mine, chunks, arrived, basis, start_row, gram_rows, copies):
    rows = chunks.shape[1]
    lines = 2 + gram_rows.shape[0]

    def kernel(mine_ref, chunks_ref, *refs):
        arrived_refs = refs[: len(arrived)]
        basis_ref, start_ref, gram_ref, piece_ref, sent_ref = refs[len(arrived) :]
        piece = chunks_ref[mine_ref[0]]
        for ref in arrived_refs:
            piece = piece + ref[0]
        piece_ref[...] = piece
        row = basis_products(piece, basis_ref, [])
        sent = jnp.concatenate([row, start_ref[...], gram_ref[...]], 0)
        sent_ref[...] = jnp.broadcast_to(sent[None], sent_ref.shape)

    args = [mine, chunks, *arrived, basis, start_row, gram_rows]
    return call(
        kernel,
        [(rows, LANES), (copies, lines, LANES)],
        args,
        [SMEM] + [VMEM] * (len(args) - 1),
    )


def inner_products(received, basis, extras, copies):
    rows = received.shape[1]

    def kernel(received_ref, basis_ref, *refs):
        extra_refs, piece_ref, row_ref = refs[: len(extras)], refs[-2], refs[-1]
        piece = jnp.sum(received_ref[...], 0)
        piece_ref[...] = piece
        row = basis_products(piece, basis_ref, [ref[...] for ref in extra_refs])
        row_ref[...] = jnp.broadcast_to(row, row_ref.shape)

    return call(kernel, [(rows, LANES), (copies, LANES)], [received, basis, *extras])


def coefficients(sums, products, size):
    lane = lax.broadcasted_iota(jnp.int32, (1, LANES), 1)
    coeffs = jnp.where(lane < size, sums, 0.0)
    squares = jnp.sum(jnp.where(lane == LANES - 1, sums, 0.0), 1, keepdims=True)
    eye = diagonal(products.shape[0])
    coeffs_col = jnp.sum(jnp.where(eye, coeffs, 0.0), 1, keepdims=True)
    combined = 2.0 * coeffs_col - jnp.sum(products * coeffs, 1, keepdims=True)
    gram_comb = jnp.sum(products * as_row(combined), 1, keepdims=True)
    squared = squares + jnp.sum(combined * (gram_comb - 2.0 * coeffs_col), 0, keepdims=True)
    squared = jnp.maximum(squared, 0.0)
    return combined, coeffs_col - gram_comb, squared, jnp.sqrt(squared + EPSILON)


def unit_lines(piece, combined, basis_ref, extra_pieces, inverse):
    kept = basis_ref.shape[0]
    spread = jnp.broadcast_to(combined[:kept], (kept, LANES))
    for e, extra in enumerate(extra_pieces):
        piece = piece - combined[kept + e : kept + e + 1] * extra
    for k in range(piece.shape[0]):
        part = jnp.sum(spread * basis_ref[:, k * LANES : (k + 1) * LANES], 0, keepdims=True)
        yield k, (piece[k : k + 1, :] - part) * inverse


def wider_gram(products, size, remaining, squared, inverse):
    shape = products.shape
    remaining = remaining * inverse
    sub_at = lax.broadcasted_iota(jnp.int32, shape, 0)
    lane_at = lax.broadcasted_iota(jnp.int32, shape, 1)
    wider = jnp.where((lane_at == size) & (sub_at < size), remaining, products)
    wider = jnp.where((sub_at == size) & (lane_at < size), as_row(remaining), wider)
    return jnp.where((sub_at == size) & (lane_at == size), squared * inverse * inverse, wider)


def first_vector(received, whole, piece, basis, total, total_right, copies):
    kept = basis.shape[0]
    rows = piece.shape[0]
    padded = kept + GROUP

    def kernel(received_ref, whole_ref, piece_ref, basis_ref, *outs):
        copies_ref, unit_ref, gram_ref, right_gram_ref, scale_ref = outs
        lines = jnp.sum(received_ref[...], 0)
        lane_at = lax.broadcasted_iota(jnp.int32, (padded, LANES), 1)
        sub_at = lax.broadcasted_iota(jnp.int32, (padded, LANES), 0)
        grams = jnp.concatenate([whole_ref[...], jnp.zeros((GROUP, LANES), jnp.float32)], 0)
        products = jnp.where(lane_at < kept, grams, 0.0)
        combined, remaining, squared, scale = coefficients(lines[0:1] * (1.0 / total), products, kept)
        inverse = 1.0 / scale
        for k, line in unit_lines(piece_ref[...], combined, basis_ref, [], inverse):
            unit_ref[pl.ds(k, 1), :] = line
            for copy in range(copies):
                copies_ref[copy, pl.ds(k, 1), :] = line
        gram_ref[...] = wider_gram(products, kept, remaining, squared, inverse)
        start_row = lines[1:2] * (1.0 / total_right)
        start_row = jnp.where(lax.broadcasted_iota(jnp.int32, (1, LANES), 1) <= kept, start_row, 0.0)
        start_row = jnp.broadcast_to(start_row, (padded, LANES))
        start_col = jnp.sum(jnp.where(lane_at == sub_at, start_row, 0.0), 1, keepdims=True)
        right = jnp.where(lane_at < kept, pltpu.roll(grams, LANES - kept, 1), 0.0)
        right = jnp.where(lane_at == kept, start_col, right)
        right_gram_ref[...] = jnp.where(sub_at == kept, start_row, right)
        scale_ref[...] = jnp.broadcast_to(scale, scale_ref.shape)

    outs = [(copies, rows, LANES), (rows, LANES), (padded, LANES), (padded, LANES), (1, LANES)]
    return call(kernel, outs, [received, whole, piece, basis])


def new_vector(received, gram, piece, basis, extras, total, copies):
    kept = basis.shape[0]
    rows = piece.shape[0]
    size = kept + len(extras)

    def kernel(received_ref, gram_ref, piece_ref, basis_ref, *refs):
        extra_refs = refs[: len(extras)]
        copies_ref, unit_ref, gram_out_ref, scale_ref = refs[len(extras) :]
        sums = jnp.sum(received_ref[...], 0, keepdims=True) * (1.0 / total)
        products = gram_ref[...]
        combined, remaining, squared, scale = coefficients(sums, products, size)
        inverse = 1.0 / scale
        extra_pieces = [ref[...] for ref in extra_refs]
        for k, line in unit_lines(piece_ref[...], combined, basis_ref, extra_pieces, inverse):
            unit_ref[pl.ds(k, 1), :] = line
            for copy in range(copies):
                copies_ref[copy, pl.ds(k, 1), :] = line
        gram_out_ref[...] = wider_gram(products, size, remaining, squared, inverse)
        scale_ref[...] = jnp.broadcast_to(scale, scale_ref.shape)

    outs = [(copies, rows, LANES), (rows, LANES), gram.shape, (1, LANES)]
    return call(kernel, outs, [received, gram, piece, basis, *extras])


def last_vector(received, gram, piece, basis, extras, total, lefts, rights, scales):
    kept = basis.shape[0]
    rows = piece.shape[0]
    left_rows = lefts[0].shape[0]
    size = kept + len(extras)
    steps = len(lefts)

    def kernel(received_ref, gram_ref, piece_ref, basis_ref, *refs):
        refs = list(refs)
        groups = []
        for members in (extras, lefts, rights, scales):
            groups.append(refs[: len(members)])
            refs = refs[len(members) :]
        extra_refs, left_refs, right_refs, scale_refs = groups
        left_out, right_out, scales_out = refs
        sums = jnp.sum(received_ref[...], 0, keepdims=True) * (1.0 / total)
        combined, _, _, scale = coefficients(sums, gram_ref[...], size)
        extra_pieces = [ref[...] for ref in extra_refs]
        for k, line in unit_lines(piece_ref[...], combined, basis_ref, extra_pieces, 1.0 / scale):
            right_out[steps - 1, :, k * LANES : (k + 1) * LANES] = line
        for step, ref in enumerate(right_refs):
            for k in range(rows):
                right_out[step, :, k * LANES : (k + 1) * LANES] = ref[k : k + 1, :]
        for step, ref in enumerate(left_refs):
            for k in range(left_rows):
                left_out[step : step + 1, k * LANES : (k + 1) * LANES] = ref[k : k + 1, :]
        values = [ref[:, 0:1] for ref in scale_refs] + [scale]
        sub_at = lax.broadcasted_iota(jnp.int32, (2, steps), 0)
        lane_at = lax.broadcasted_iota(jnp.int32, (2, steps), 1)
        table = jnp.zeros((2, steps), jnp.float32)
        for at, value in enumerate(values):
            table = jnp.where((sub_at == at % 2) & (lane_at == at // 2), value, table)
        scales_out[...] = table

    outs = [(steps, left_rows * LANES), (steps, 1, rows * LANES), (2, steps)]
    return call(kernel, outs, [received, gram, piece, basis, *extras, *lefts, *rights, *scales])


def shards(tiles, tile_index, u_basis, v_basis, v_start):
    blocks = tiles[0]
    slots = tile_index[0]
    width = blocks.shape[1]
    cols_len = v_start.shape[0]
    col_blocks = cols_len // width
    row_count = lax.axis_size("row")
    col_count = lax.axis_size("col")
    devices = row_count * col_count
    kept = u_basis.shape[0]
    left_piece = u_basis.shape[1]
    right_piece = v_basis.shape[2]
    rows_len = left_piece * col_count
    row_blocks = rows_len // width
    left_rows = left_piece // width
    right_rows = right_piece // width
    total_left = rows_len * row_count
    total_right = cols_len * col_count

    whole_start = v_start.reshape(col_blocks, width)
    dense = multiply_tiles(blocks, slots, whole_start, col_blocks, row_blocks, True)
    chunks = dense.reshape(col_count, left_rows, width)
    mine = lax.axis_index("col")
    arrived = []
    for shift in range(1, col_count):
        pairs = [(i, (i + shift) % col_count) for i in range(col_count)]
        chunk = lax.dynamic_index_in_dim(chunks, (mine + shift) % col_count, 0, True)
        arrived.append(lax.ppermute(chunk, "col", pairs))

    right_basis = v_basis[:, 0, :]
    start_share = lax.dynamic_slice_in_dim(
        whole_start, lax.axis_index("row") * right_rows, right_rows, 0
    )
    grams, start_row = first_grams(
        u_basis, right_basis, start_share, dense, total_left, total_right
    )
    chunk = grams.size // devices
    chunk_rows = -(-chunk // LANES)
    gram_rows = jnp.sum(swap(grams.reshape(devices, chunk), BOTH), 0)
    gram_rows = jnp.pad(gram_rows, (0, chunk_rows * LANES - chunk)).reshape(chunk_rows, LANES)

    lefts, rights, scales = ([], [], [])
    right_extras = [start_share]
    received = None
    for iteration in range(ITERS):
        if iteration == 0:
            piece, sent = first_products(
                mine.reshape(1), chunks, arrived, u_basis, start_row, gram_rows, devices
            )
            everything = swap(sent, BOTH)
            whole = everything[:, 2:, :].reshape(devices, chunk_rows * LANES)[:, :chunk]
            copies, left_unit, left_gram, right_gram, alpha = first_vector(
                everything, whole.reshape(grams.shape), piece, u_basis, total_left, total_right, col_count
            )
        else:
            piece, row = inner_products(received, u_basis, lefts, devices)
            summed_rows = swap(row.reshape(devices, 1, LANES), BOTH).reshape(devices, LANES)
            copies, left_unit, left_gram, alpha = new_vector(
                summed_rows, left_gram, piece, u_basis, lefts, total_left, col_count
            )
        lefts = lefts + [left_unit]
        scales = scales + [alpha]
        joined = swap(copies, "col").reshape(row_blocks, width)
        dense = multiply_tiles(blocks, slots, joined, row_blocks, col_blocks, False)
        received = swap(dense.reshape(row_count, right_rows, width), "row")
        piece, row = inner_products(received, right_basis, right_extras, devices)
        summed_rows = swap(row.reshape(devices, 1, LANES), BOTH).reshape(devices, LANES)
        if iteration + 1 < ITERS:
            copies, right_unit, right_gram, beta = new_vector(
                summed_rows, right_gram, piece, right_basis, right_extras, total_right, row_count
            )
            rights = rights + [right_unit]
            right_extras = right_extras + [right_unit]
            scales = scales + [beta]
            joined = swap(copies, "row").reshape(col_blocks, width)
            dense = multiply_tiles(blocks, slots, joined, col_blocks, row_blocks, True)
            received = swap(dense.reshape(col_count, left_rows, width), "col")
    return last_vector(
        summed_rows, right_gram, piece, right_basis, right_extras, total_right, lefts, rights, scales
    )


def solution(mesh):
    placed = (
        P("row", "col", None, None),
        P("row", "col"),
        P(None, ("row", "col")),
        P(None, "col", "row"),
        P("col"),
    )
    return jax.shard_map(
        shards,
        mesh=mesh,
        in_specs=placed,
        out_specs=(P(None, ("row", "col")), P(None, "col", "row"), P()),
        check_vma=False,
    )
```

```python
import jax
import jax.numpy as jnp
from jax import lax
from jax.experimental import pallas as pl
from jax.experimental.pallas import tpu as pltpu
from jax.sharding import PartitionSpec as P

ITERS = 2


HIGHEST = lax.Precision.HIGHEST
EPSILON = 1e-06
BOTH = ("row", "col")
LANES = 128
GROUP = 8
PARAMS = pltpu.CompilerParams(vmem_limit_bytes=8 * 2**20)
VMEM = pl.BlockSpec(memory_space=pltpu.VMEM)
SMEM = pl.BlockSpec(memory_space=pltpu.SMEM)
ANY = pl.BlockSpec(memory_space=pl.ANY)


def swap(chunks, axis):
    return lax.all_to_all(chunks, axis, 0, 0, tiled=True)


def call(kernel, outs, args, specs=None, scratch=()):
    shapes = tuple(jax.ShapeDtypeStruct(shape, jnp.float32) for shape in outs)
    return pl.pallas_call(
        kernel,
        out_shape=shapes,
        in_specs=specs or [VMEM] * len(args),
        out_specs=tuple([VMEM] * len(outs)),
        scratch_shapes=list(scratch),
        compiler_params=PARAMS,
    )(*args)


def take(refs, *counts):
    refs = list(refs)
    groups = []
    for count in counts:
        groups.append(refs[:count])
        refs = refs[count:]
    return groups + [refs]


def exchange(messages, axis):
    count = lax.axis_size(axis)
    arrived = [messages[0]]
    for x in range(1, count):
        arrived.append(lax.ppermute(messages[x], axis, [(i, i ^ x) for i in range(count)]))
    return arrived


def three_parts(x):
    high = x.astype(jnp.bfloat16)
    rest = x - high.astype(jnp.float32)
    middle = rest.astype(jnp.bfloat16)
    low = (rest - middle.astype(jnp.float32)).astype(jnp.bfloat16)
    return jnp.concatenate([high, middle, low], 0)


def diagonal(rows):
    shape = (rows, LANES)
    return lax.broadcasted_iota(jnp.int32, shape, 0) == lax.broadcasted_iota(jnp.int32, shape, 1)


def as_row(column):
    return jnp.sum(jnp.where(diagonal(column.shape[0]), column, 0.0), 0, keepdims=True)


def total_sum(x):
    return jnp.sum(jnp.sum(x, 0, keepdims=True), 1, keepdims=True)


def tile_sums(slots_ref, tiles_ref, vector_ref, dense_ref, picked_ref, product_ref, divisor, is_forward):
    count = tiles_ref.shape[0]
    limit = vector_ref.shape[0] * dense_ref.shape[0]
    contract = (((1,), (1,)), ((), ())) if is_forward else (((1,), (0,)), ((), ()))
    targets = []
    for t in range(count):
        slot = slots_ref[t]
        live = slot < limit
        slot = jnp.where(live, slot, 0)
        row = lax.div(slot, divisor)
        column = slot - row * divisor
        targets.append(row if is_forward else column)
        line = vector_ref[pl.ds(column if is_forward else row, 1), :]
        picked_ref[pl.ds(t, 1), :] = jnp.where(live, line, 0.0)
    parts = three_parts(picked_ref[...])
    dense_ref[...] = jnp.zeros_like(dense_ref)
    for t in range(count):
        result = lax.dot_general(parts, tiles_ref[t], contract, preferred_element_type=jnp.float32)
        product_ref[pl.ds(t, 1), :] = (
            result[t : t + 1]
            + result[count + t : count + t + 1]
            + result[2 * count + t : 2 * count + t + 1]
        )
    for t in range(count):
        line = pl.ds(targets[t], 1)
        dense_ref[line, :] = dense_ref[line, :] + product_ref[pl.ds(t, 1), :]


def packed_gram(basis, total):
    gram = lax.dot_general(
        basis,
        basis,
        (((1,), (1,)), ((), ())),
        precision=HIGHEST,
        preferred_element_type=jnp.float32,
    )
    half = gram.shape[0] // 2
    return gram[:half] * (1.0 / total), gram[half:] * (1.0 / total)


def unpacked_gram(packed, padded):
    half = packed.shape[0]
    grams = jnp.concatenate(
        [
            packed,
            pltpu.roll(packed, LANES // 2, 1),
            jnp.zeros((padded - 2 * half, LANES), jnp.float32),
        ],
        0,
    )
    lane_at = lax.broadcasted_iota(jnp.int32, grams.shape, 1)
    return jnp.where(lane_at < 2 * half, grams, 0.0)


def start(mine, tiles, slots, vector, basis, row_blocks, total, peers):
    count, width = tiles.shape[0], tiles.shape[1]
    divisor = vector.shape[0]
    kept = basis.shape[0]
    rows = row_blocks // peers
    share = kept * kept // LANES // peers

    def kernel(mine_ref, slots_ref, tiles_hbm, vector_hbm, basis_hbm, *refs):
        outs, scratch = take(refs, peers)
        tiles_ref, vector_ref, basis_ref, dense_ref, packed_ref, picked_ref, product_ref, sems = scratch
        moves = [
            pltpu.make_async_copy(source, target, sems.at[at])
            for at, (source, target) in enumerate(
                ((vector_hbm, vector_ref), (tiles_hbm, tiles_ref), (basis_hbm, basis_ref))
            )
        ]
        for move in moves:
            move.start()
        moves[0].wait()
        moves[1].wait()
        tile_sums(slots_ref, tiles_ref, vector_ref, dense_ref, picked_ref, product_ref, divisor, True)
        moves[2].wait()
        upper, lower = packed_gram(basis_ref[...], total)
        packed_ref[:, :kept] = upper
        packed_ref[:, kept:] = lower
        for x, out in enumerate(outs):
            peer = jnp.bitwise_xor(mine_ref[0], x)
            out[:rows, :] = dense_ref[pl.ds(peer * rows, rows), :]
            out[rows:, :] = packed_ref[pl.ds(peer * share, share), :]

    scratch = [
        pltpu.VMEM(tiles.shape, tiles.dtype),
        pltpu.VMEM(vector.shape, jnp.float32),
        pltpu.VMEM(basis.shape, jnp.float32),
        pltpu.VMEM((row_blocks, width), jnp.float32),
        pltpu.VMEM((kept // 2, 2 * kept), jnp.float32),
        pltpu.VMEM((count, width), jnp.float32),
        pltpu.VMEM((count, width), jnp.float32),
        pltpu.SemaphoreType.DMA((3,)),
    ]
    return call(
        kernel,
        [(rows + share, width)] * peers,
        [mine, slots, tiles, vector, basis],
        [SMEM, SMEM, ANY, ANY, ANY],
        scratch,
    )


def right_start(mine_row, v_basis, vector, after, total):
    kept, _, length = v_basis.shape
    rows = length // LANES

    def kernel(mine_ref, basis_ref, vector_ref, after_ref, flat_ref, piece_ref, row_ref, packed_ref):
        for k in range(rows):
            at = slice(k * LANES, (k + 1) * LANES)
            flat_ref[:, at] = basis_ref[:, 0, at]
        piece = vector_ref[pl.ds(mine_ref[0] * rows, rows), :]
        piece_ref[...] = piece
        row_ref[...] = basis_products(piece, flat_ref, [piece])
        upper, lower = packed_gram(flat_ref[...], total)
        packed_ref[:, :kept] = upper
        packed_ref[:, kept:] = lower

    return call(
        kernel,
        [(kept, length), (rows, LANES), (1, LANES), (kept // 2, 2 * kept)],
        [mine_row, v_basis, vector, after],
        [SMEM, VMEM, VMEM, VMEM],
    )


def forward_messages(mine, tiles, slots, vector, row_blocks, peers):
    count, width = tiles.shape[0], tiles.shape[1]
    divisor = vector.shape[0]
    rows = row_blocks // peers

    def kernel(mine_ref, slots_ref, tiles_ref, vector_ref, *refs):
        outs, (dense_ref, picked_ref, product_ref) = take(refs, peers)
        tile_sums(slots_ref, tiles_ref, vector_ref, dense_ref, picked_ref, product_ref, divisor, True)
        for x, out in enumerate(outs):
            peer = jnp.bitwise_xor(mine_ref[0], x)
            out[...] = dense_ref[pl.ds(peer * rows, rows), :]

    scratch = [pltpu.VMEM((row_blocks, width), jnp.float32)]
    scratch += [pltpu.VMEM((count, width), jnp.float32)] * 2
    return call(
        kernel,
        [(rows, width)] * peers,
        [mine, slots, tiles, vector],
        [SMEM, SMEM, VMEM, VMEM],
        scratch,
    )


def backward_product(mine, tiles, slots, messages, rows, col_blocks):
    count, width = tiles.shape[0], tiles.shape[1]
    peers = len(messages)
    share = messages[0].shape[0] - rows

    def kernel(mine_ref, slots_ref, tiles_ref, *refs):
        sources, rest = take(refs, peers)
        outs, (vector_ref, picked_ref, product_ref) = take(rest, 2 if share else 1)
        for x, source in enumerate(sources):
            peer = jnp.bitwise_xor(mine_ref[0], x)
            vector_ref[pl.ds(peer * rows, rows), :] = source[:rows, :]
        tile_sums(
            slots_ref, tiles_ref, vector_ref, outs[0], picked_ref, product_ref, col_blocks, False
        )
        if share:
            added = sources[0][rows:, :]
            for source in sources[1:]:
                added = added + source[rows:, :]
            outs[1][...] = added

    scratch = [pltpu.VMEM((rows * peers, width), jnp.float32)]
    scratch += [pltpu.VMEM((count, width), jnp.float32)] * 2
    outs = [(col_blocks, width)] + ([(share, width)] if share else [])
    return call(
        kernel,
        outs,
        [mine, slots, tiles, *messages],
        [SMEM, SMEM] + [VMEM] * (1 + peers),
        scratch,
    )


def basis_products(piece, basis_ref, extra_pieces):
    kept = basis_ref.shape[0]
    total = jnp.zeros((kept, LANES), jnp.float32)
    for k in range(piece.shape[0]):
        total = total + basis_ref[:, k * LANES : (k + 1) * LANES] * piece[k : k + 1, :]
    row = as_row(jnp.sum(total, 1, keepdims=True))
    lane = lax.broadcasted_iota(jnp.int32, (1, LANES), 1)
    for e, extra in enumerate(extra_pieces):
        row = row + jnp.where(lane == kept + e, total_sum(extra * piece), 0.0)
    return row + jnp.where(lane == LANES - 1, total_sum(piece * piece), 0.0)


def inner_products(pieces, rows, basis, extras, riders, copies):
    listed = pieces if isinstance(pieces, (list, tuple)) else [pieces]
    stacked = listed is not pieces
    further = 0 if stacked else listed[0].shape[0] - rows
    lines = 1 + further + sum(rider.shape[0] for rider in riders)

    def kernel(*refs):
        sources, (basis_ref,), extra_refs, rider_refs, (piece_ref, sent_ref) = take(
            refs, len(listed), 1, len(extras), len(riders)
        )
        if stacked:
            summed = jnp.sum(sources[0][...], 0)
        else:
            summed = sources[0][...]
            for source in sources[1:]:
                summed = summed + source[...]
        piece = summed[:rows]
        piece_ref[...] = piece
        sent = [basis_products(piece, basis_ref, [ref[...] for ref in extra_refs])]
        sent += [summed[rows + k : rows + k + 1] for k in range(further)]
        for ref in rider_refs:
            sent += [ref[k : k + 1, :] for k in range(ref.shape[0])]
        for at, line in enumerate(sent):
            shape = (copies, 1, LANES)
            sent_ref[:, :, at * LANES : (at + 1) * LANES] = jnp.broadcast_to(line[None], shape)

    return call(
        kernel,
        [(rows, LANES), (copies, 1, lines * LANES)],
        [*listed, basis, *extras, *riders],
    )


def received_row(received_ref, at):
    lines = received_ref[:, 0, at * LANES : (at + 1) * LANES]
    return jnp.sum(lines, 0, keepdims=True)


def received_gram(received_ref, first, packed_ref, peers):
    share = packed_ref.shape[0] // peers
    devices = received_ref.shape[0]
    for k in range(share):
        at = slice((first + k) * LANES, (first + k + 1) * LANES)
        added = received_ref[0:peers, 0, at]
        for i in range(1, devices // peers):
            added = added + received_ref[i * peers : (i + 1) * peers, 0, at]
        for peer in range(peers):
            packed_ref[peer * share + k : peer * share + k + 1, :] = added[peer : peer + 1]


def first_vector(mine, received, piece, basis, right_packed, total, peers):
    kept = basis.shape[0]
    rows = piece.shape[0]
    padded = kept + GROUP
    share = right_packed.shape[0] // peers

    def kernel(mine_ref, received_ref, piece_ref, basis_ref, right_ref, *refs):
        messages, (unit_ref, gram_ref, scale_ref, packed_ref) = take(refs, peers)
        received_gram(received_ref, 1, packed_ref, peers)
        products = unpacked_gram(packed_ref[...], padded)
        sums = received_row(received_ref, 0) * (1.0 / total)
        combined, remaining, squared, scale = coefficients(sums, products, kept)
        inverse = 1.0 / scale
        for k, line in unit_lines(piece_ref[...], combined, basis_ref, [], inverse):
            unit_ref[pl.ds(k, 1), :] = line
            for message in messages:
                message[pl.ds(k, 1), :] = line
        for x, message in enumerate(messages):
            peer = jnp.bitwise_xor(mine_ref[0], x)
            message[rows:, :] = right_ref[pl.ds(peer * share, share), :]
        gram_ref[...] = wider_gram(products, kept, remaining, squared, inverse)
        scale_ref[...] = jnp.broadcast_to(scale, scale_ref.shape)

    outs = [(rows + share, LANES)] * peers + [(rows, LANES), (padded, LANES), (1, LANES)]
    return call(
        kernel,
        outs,
        [mine, received, piece, basis, right_packed],
        [SMEM] + [VMEM] * 4,
        [pltpu.VMEM(right_packed.shape, jnp.float32)],
    )


def new_vector(received, gram, piece, basis, extras, total, copies, peers, widen):
    kept = basis.shape[0]
    rows = piece.shape[0]
    size = kept + len(extras)
    padded = kept + GROUP
    grams = [] if gram is None else [gram]

    def kernel(received_ref, piece_ref, basis_ref, *refs):
        gram_refs, extra_refs, rest = take(refs, len(grams), len(extras))
        copies_refs, (unit_ref, scale_ref), wider_refs, scratch = take(
            rest, 1 if copies else 0, 2, 1 if widen else 0
        )
        if gram_refs:
            products = gram_refs[0][...]
        else:
            received_gram(received_ref, 2, scratch[0], peers)
            products = unpacked_gram(scratch[0][...], padded)
            lane_at = lax.broadcasted_iota(jnp.int32, (padded, LANES), 1)
            sub_at = lax.broadcasted_iota(jnp.int32, (padded, LANES), 0)
            row = received_row(received_ref, 1) * (1.0 / total)
            row = jnp.broadcast_to(row, (padded, LANES))
            column = jnp.sum(jnp.where(lane_at == sub_at, row, 0.0), 1, keepdims=True)
            products = jnp.where((lane_at == kept) & (sub_at <= kept), column, products)
            products = jnp.where((sub_at == kept) & (lane_at <= kept), row, products)
        sums = received_row(received_ref, 0) * (1.0 / total)
        combined, remaining, squared, scale = coefficients(sums, products, size)
        inverse = 1.0 / scale
        extra_pieces = [ref[...] for ref in extra_refs]
        for k, line in unit_lines(piece_ref[...], combined, basis_ref, extra_pieces, inverse):
            unit_ref[pl.ds(k, 1), :] = line
            for ref in copies_refs:
                for copy in range(copies):
                    ref[copy, pl.ds(k, 1), :] = line
        for ref in wider_refs:
            ref[...] = wider_gram(products, size, remaining, squared, inverse)
        scale_ref[...] = jnp.broadcast_to(scale, scale_ref.shape)

    outs = [(copies, rows, LANES)] if copies else []
    outs += [(rows, LANES), (1, LANES)] + ([(padded, LANES)] if widen else [])
    scratch = [] if grams else [pltpu.VMEM((kept // 2, LANES), jnp.float32)]
    return call(kernel, outs, [received, piece, basis, *grams, *extras], None, scratch)


def coefficients(sums, products, size):
    lane = lax.broadcasted_iota(jnp.int32, (1, LANES), 1)
    coeffs = jnp.where(lane < size, sums, 0.0)
    squares = jnp.sum(jnp.where(lane == LANES - 1, sums, 0.0), 1, keepdims=True)
    eye = diagonal(products.shape[0])
    coeffs_col = jnp.sum(jnp.where(eye, coeffs, 0.0), 1, keepdims=True)
    combined = 2.0 * coeffs_col - jnp.sum(products * coeffs, 1, keepdims=True)
    gram_comb = jnp.sum(products * as_row(combined), 1, keepdims=True)
    squared = squares + jnp.sum(combined * (gram_comb - 2.0 * coeffs_col), 0, keepdims=True)
    squared = jnp.maximum(squared, 0.0)
    return combined, coeffs_col - gram_comb, squared, jnp.sqrt(squared + EPSILON)


def unit_lines(piece, combined, basis_ref, extra_pieces, inverse):
    kept = basis_ref.shape[0]
    spread = jnp.broadcast_to(combined[:kept], (kept, LANES))
    for e, extra in enumerate(extra_pieces):
        piece = piece - combined[kept + e : kept + e + 1] * extra
    for k in range(piece.shape[0]):
        part = jnp.sum(spread * basis_ref[:, k * LANES : (k + 1) * LANES], 0, keepdims=True)
        yield k, (piece[k : k + 1, :] - part) * inverse


def wider_gram(products, size, remaining, squared, inverse):
    shape = products.shape
    remaining = remaining * inverse
    sub_at = lax.broadcasted_iota(jnp.int32, shape, 0)
    lane_at = lax.broadcasted_iota(jnp.int32, shape, 1)
    wider = jnp.where((lane_at == size) & (sub_at < size), remaining, products)
    wider = jnp.where((sub_at == size) & (lane_at < size), as_row(remaining), wider)
    return jnp.where((sub_at == size) & (lane_at == size), squared * inverse * inverse, wider)


def last_vector(received, gram, piece, basis, extras, total, lefts, rights, scales):
    kept = basis.shape[0]
    rows = piece.shape[0]
    left_rows = lefts[0].shape[0]
    size = kept + len(extras)
    steps = len(lefts)

    def kernel(received_ref, gram_ref, piece_ref, basis_ref, *refs):
        extra_refs, left_refs, right_refs, scale_refs, outs = take(
            refs, len(extras), len(lefts), len(rights), len(scales)
        )
        left_out, right_out, scales_out = outs
        sums = received_row(received_ref, 0) * (1.0 / total)
        combined, _, _, scale = coefficients(sums, gram_ref[...], size)
        extra_pieces = [ref[...] for ref in extra_refs]
        for k, line in unit_lines(piece_ref[...], combined, basis_ref, extra_pieces, 1.0 / scale):
            right_out[steps - 1, :, k * LANES : (k + 1) * LANES] = line
        for step, ref in enumerate(right_refs):
            for k in range(rows):
                right_out[step, :, k * LANES : (k + 1) * LANES] = ref[k : k + 1, :]
        for step, ref in enumerate(left_refs):
            for k in range(left_rows):
                left_out[step : step + 1, k * LANES : (k + 1) * LANES] = ref[k : k + 1, :]
        values = [ref[:, 0:1] for ref in scale_refs] + [scale]
        sub_at = lax.broadcasted_iota(jnp.int32, (2, steps), 0)
        lane_at = lax.broadcasted_iota(jnp.int32, (2, steps), 1)
        table = jnp.zeros((2, steps), jnp.float32)
        for at, value in enumerate(values):
            table = jnp.where((sub_at == at % 2) & (lane_at == at // 2), value, table)
        scales_out[...] = table

    outs = [(steps, left_rows * LANES), (steps, 1, rows * LANES), (2, steps)]
    return call(kernel, outs, [received, gram, piece, basis, *extras, *lefts, *rights, *scales])


def shards(tiles, tile_index, u_basis, v_basis, v_start):
    blocks = tiles[0]
    slots = tile_index[0]
    width = blocks.shape[1]
    cols_len = v_start.shape[0]
    col_blocks = cols_len // width
    row_count = lax.axis_size("row")
    col_count = lax.axis_size("col")
    devices = row_count * col_count
    left_piece = u_basis.shape[1]
    right_piece = v_basis.shape[2]
    rows_len = left_piece * col_count
    row_blocks = rows_len // width
    left_rows = left_piece // width
    right_rows = right_piece // width
    total_left = rows_len * row_count
    total_right = cols_len * col_count
    mine = lax.axis_index("col").reshape(1)
    mine_row = lax.axis_index("row").reshape(1)

    whole_start = v_start.reshape(col_blocks, width)
    messages = start(mine, blocks, slots, whole_start, u_basis, row_blocks, total_left, col_count)
    right_basis, start_share, start_row, right_packed = right_start(
        mine_row, v_basis, whole_start, messages[0], total_right
    )
    arrived = exchange(messages, "col")

    lefts, rights, scales = ([], [], [])
    right_extras = [start_share]
    left_gram = right_gram = None
    for iteration in range(ITERS):
        last = iteration + 1 == ITERS
        piece, sent = inner_products(arrived, left_rows, u_basis, lefts, [], devices)
        summed_rows = swap(sent, BOTH)
        if iteration == 0:
            *messages, left_unit, left_gram, alpha = first_vector(
                mine, summed_rows, piece, u_basis, right_packed, total_left, col_count
            )
        else:
            left_unit, alpha, *wider = new_vector(
                summed_rows, left_gram, piece, u_basis, lefts, total_left, 0, col_count, not last
            )
            left_gram = wider[0] if wider else None
            messages = [left_unit] * col_count
        lefts = lefts + [left_unit]
        scales = scales + [alpha]
        arrived = exchange(messages, "col")
        dense, *further = backward_product(mine, blocks, slots, arrived, left_rows, col_blocks)
        received = swap(dense.reshape(row_count, right_rows, width), "row")
        riders = [start_row, *further] if iteration == 0 else []
        piece, sent = inner_products(received, right_rows, right_basis, right_extras, riders, devices)
        summed_rows = swap(sent, BOTH)
        if not last:
            copies, right_unit, beta, right_gram = new_vector(
                summed_rows,
                right_gram,
                piece,
                right_basis,
                right_extras,
                total_right,
                row_count,
                col_count,
                True,
            )
            rights = rights + [right_unit]
            right_extras = right_extras + [right_unit]
            scales = scales + [beta]
            joined = swap(copies, "row").reshape(col_blocks, width)
            messages = forward_messages(mine, blocks, slots, joined, row_blocks, col_count)
            arrived = exchange(messages, "col")
    return last_vector(
        summed_rows, right_gram, piece, right_basis, right_extras, total_right, lefts, rights, scales
    )


def solution(mesh):
    placed = (
        P("row", "col", None, None),
        P("row", "col"),
        P(None, ("row", "col")),
        P(None, "col", "row"),
        P("col"),
    )
    return jax.shard_map(
        shards,
        mesh=mesh,
        in_specs=placed,
        out_specs=(P(None, ("row", "col")), P(None, "col", "row"), P()),
        check_vma=False,
    )
```

```python
import jax
import jax.numpy as jnp
from jax import lax
from jax.experimental import pallas as pl
from jax.experimental.pallas import tpu as pltpu
from jax.sharding import PartitionSpec as P

ITERS = 2


HIGHEST = lax.Precision.HIGHEST
EPSILON = 1e-06
BOTH = ("row", "col")
LANES = 128
GROUP = 8
PARAMS = pltpu.CompilerParams(vmem_limit_bytes=8 * 2**20)
WIDE = pltpu.CompilerParams(vmem_limit_bytes=63950 * 2**10)
VMEM = pl.BlockSpec(memory_space=pltpu.VMEM)
SMEM = pl.BlockSpec(memory_space=pltpu.SMEM)
HBM = pl.BlockSpec(memory_space=pltpu.HBM)


def swap(chunks, axis):
    return lax.all_to_all(chunks, axis, 0, 0, tiled=True)


def call(kernel, outs, args, specs=None, scratch=(), params=PARAMS):
    shapes = tuple(jax.ShapeDtypeStruct(shape, jnp.float32) for shape in outs)
    return pl.pallas_call(
        kernel,
        out_shape=shapes,
        in_specs=specs or [VMEM] * len(args),
        out_specs=tuple([VMEM] * len(outs)),
        scratch_shapes=list(scratch),
        compiler_params=params,
    )(*args)


def take(refs, *counts):
    refs = list(refs)
    groups = []
    for count in counts:
        groups.append(refs[:count])
        refs = refs[count:]
    return groups + [refs]


def exchange(messages, hops, axis):
    count = lax.axis_size(axis)
    arrived = [messages[0]]
    for x in hops:
        arrived.append(lax.ppermute(messages[x], axis, [(i, i ^ x) for i in range(count)]))
    return arrived


def three_parts(x):
    high = x.astype(jnp.bfloat16)
    rest = x - high.astype(jnp.float32)
    middle = rest.astype(jnp.bfloat16)
    low = (rest - middle.astype(jnp.float32)).astype(jnp.bfloat16)
    return jnp.concatenate([high, middle, low], 0)


def diagonal(rows):
    shape = (rows, LANES)
    return lax.broadcasted_iota(jnp.int32, shape, 0) == lax.broadcasted_iota(jnp.int32, shape, 1)


def as_row(column):
    return jnp.sum(jnp.where(diagonal(column.shape[0]), column, 0.0), 0, keepdims=True)


def total_sum(x):
    return jnp.sum(jnp.sum(x, 0, keepdims=True), 1, keepdims=True)


def tile_sums(slots_ref, tiles_ref, vector_ref, dense_ref, picked_ref, product_ref, divisor, is_forward):
    count = tiles_ref.shape[0]
    limit = vector_ref.shape[0] * dense_ref.shape[0]
    contract = (((1,), (1,)), ((), ())) if is_forward else (((1,), (0,)), ((), ()))
    targets = []
    for t in range(count):
        slot = slots_ref[t]
        live = slot < limit
        slot = jnp.where(live, slot, 0)
        row = lax.div(slot, divisor)
        column = slot - row * divisor
        targets.append(row if is_forward else column)
        line = vector_ref[pl.ds(column if is_forward else row, 1), :]
        picked_ref[pl.ds(t, 1), :] = jnp.where(live, line, 0.0)
    parts = three_parts(picked_ref[...])
    dense_ref[...] = jnp.zeros_like(dense_ref)
    for t in range(count):
        result = lax.dot_general(parts, tiles_ref[t], contract, preferred_element_type=jnp.float32)
        product_ref[pl.ds(t, 1), :] = (
            result[t : t + 1]
            + result[count + t : count + t + 1]
            + result[2 * count + t : 2 * count + t + 1]
        )
    for t in range(count):
        line = pl.ds(targets[t], 1)
        dense_ref[line, :] = dense_ref[line, :] + product_ref[pl.ds(t, 1), :]


def packed_gram(basis, total):
    gram = lax.dot_general(
        basis,
        basis,
        (((1,), (1,)), ((), ())),
        precision=HIGHEST,
        preferred_element_type=jnp.float32,
    )
    half = gram.shape[0] // 2
    return gram[:half] * (1.0 / total), gram[half:] * (1.0 / total)


def unpacked_gram(packed, padded):
    half = packed.shape[0]
    grams = jnp.concatenate(
        [
            packed,
            pltpu.roll(packed, LANES // 2, 1),
            jnp.zeros((padded - 2 * half, LANES), jnp.float32),
        ],
        0,
    )
    lane_at = lax.broadcasted_iota(jnp.int32, grams.shape, 1)
    return jnp.where(lane_at < 2 * half, grams, 0.0)


def start(mine, tiles, slots, vector, basis, row_blocks, total, peers):
    count, width = tiles.shape[0], tiles.shape[1]
    divisor = vector.shape[0]
    kept = basis.shape[0]
    rows = row_blocks // peers
    share = kept * kept // LANES // peers

    def kernel(mine_ref, slots_ref, tiles_hbm, vector_hbm, basis_hbm, *refs):
        outs, scratch = take(refs, peers)
        tiles_ref, vector_ref, basis_ref, dense_ref, packed_ref, picked_ref, product_ref, sems = scratch
        moves = [
            pltpu.make_async_copy(source, target, sems.at[at])
            for at, (source, target) in enumerate(
                ((vector_hbm, vector_ref), (tiles_hbm, tiles_ref), (basis_hbm, basis_ref))
            )
        ]
        for move in moves:
            move.start()
        moves[0].wait()
        moves[1].wait()
        tile_sums(slots_ref, tiles_ref, vector_ref, dense_ref, picked_ref, product_ref, divisor, True)
        moves[2].wait()
        upper, lower = packed_gram(basis_ref[...], total)
        packed_ref[:, :kept] = upper
        packed_ref[:, kept:] = lower
        for x, out in enumerate(outs):
            peer = jnp.bitwise_xor(mine_ref[0], x)
            out[:rows, :] = dense_ref[pl.ds(peer * rows, rows), :]
            out[rows:, :] = packed_ref[pl.ds(peer * share, share), :]

    scratch = [
        pltpu.VMEM(tiles.shape, tiles.dtype),
        pltpu.VMEM(vector.shape, jnp.float32),
        pltpu.VMEM(basis.shape, jnp.float32),
        pltpu.VMEM((row_blocks, width), jnp.float32),
        pltpu.VMEM((kept // 2, 2 * kept), jnp.float32),
        pltpu.VMEM((count, width), jnp.float32),
        pltpu.VMEM((count, width), jnp.float32),
        pltpu.SemaphoreType.DMA((3,)),
    ]
    return call(
        kernel,
        [(rows + share, width)] * peers,
        [mine, slots, tiles, vector, basis],
        [SMEM, SMEM, HBM, HBM, HBM],
        scratch,
        WIDE,
    )


def right_start(mine_row, v_basis, vector, after, total):
    kept, _, length = v_basis.shape
    rows = length // LANES

    def kernel(mine_ref, basis_ref, vector_ref, after_ref, flat_ref, piece_ref, row_ref, packed_ref):
        for k in range(rows):
            at = slice(k * LANES, (k + 1) * LANES)
            flat_ref[:, at] = basis_ref[:, 0, at]
        piece = vector_ref[pl.ds(mine_ref[0] * rows, rows), :]
        piece_ref[...] = piece
        row_ref[...] = basis_products(piece, flat_ref, [piece])
        upper, lower = packed_gram(flat_ref[...], total)
        packed_ref[:, :kept] = upper
        packed_ref[:, kept:] = lower

    return call(
        kernel,
        [(kept, length), (rows, LANES), (1, LANES), (kept // 2, 2 * kept)],
        [mine_row, v_basis, vector, after],
        [SMEM, VMEM, VMEM, VMEM],
    )


def forward_messages(mine, tiles, slots, vector, row_blocks, peers):
    count, width = tiles.shape[0], tiles.shape[1]
    divisor = vector.shape[0]
    rows = row_blocks // peers

    def kernel(mine_ref, slots_ref, tiles_ref, vector_ref, *refs):
        outs, (dense_ref, picked_ref, product_ref) = take(refs, peers)
        tile_sums(slots_ref, tiles_ref, vector_ref, dense_ref, picked_ref, product_ref, divisor, True)
        for x, out in enumerate(outs):
            peer = jnp.bitwise_xor(mine_ref[0], x)
            out[...] = dense_ref[pl.ds(peer * rows, rows), :]

    scratch = [pltpu.VMEM((row_blocks, width), jnp.float32)]
    scratch += [pltpu.VMEM((count, width), jnp.float32)] * 2
    return call(
        kernel,
        [(rows, width)] * peers,
        [mine, slots, tiles, vector],
        [SMEM, SMEM, VMEM, VMEM],
        scratch,
    )


def backward_product(mine, tiles, slots, messages, hops, rows, col_blocks, peers_row):
    count, width = tiles.shape[0], tiles.shape[1]
    peers = len(messages)
    share = messages[0].shape[0] - rows
    chunk = col_blocks // peers_row
    joined = share // peers_row if share % peers_row == 0 else 0
    apart = share and not joined

    def kernel(mine_ref, slots_ref, tiles_ref, *refs):
        sources, rest = take(refs, peers)
        (chunks_ref,), apart_refs, scratch = take(rest, 1, 1 if apart else 0)
        vector_ref, dense_ref, picked_ref, product_ref = scratch
        for at, source in enumerate(sources):
            peer = jnp.bitwise_xor(mine_ref[0], ([0] + hops)[at])
            vector_ref[pl.ds(peer * rows, rows), :] = source[:rows, :]
        tile_sums(
            slots_ref, tiles_ref, vector_ref, dense_ref, picked_ref, product_ref, col_blocks, False
        )
        for i in range(peers_row):
            chunks_ref[i, :chunk, :] = dense_ref[i * chunk : (i + 1) * chunk, :]
        if share:
            added = sources[0][rows:, :]
            for source in sources[1:]:
                added = added + source[rows:, :]
            for ref in apart_refs:
                ref[...] = added
            if joined:
                for i in range(peers_row):
                    chunks_ref[i, chunk:, :] = added[i * joined : (i + 1) * joined]

    scratch = [pltpu.VMEM((rows * peers, width), jnp.float32)]
    scratch += [pltpu.VMEM((col_blocks, width), jnp.float32)]
    scratch += [pltpu.VMEM((count, width), jnp.float32)] * 2
    outs = [(peers_row, chunk + joined, width)] + ([(share, width)] if apart else [])
    return call(
        kernel,
        outs,
        [mine, slots, tiles, *messages],
        [SMEM, SMEM] + [VMEM] * (1 + peers),
        scratch,
    )


def basis_products(piece, basis_ref, extra_pieces):
    kept = basis_ref.shape[0]
    total = jnp.zeros((kept, LANES), jnp.float32)
    for k in range(piece.shape[0]):
        total = total + basis_ref[:, k * LANES : (k + 1) * LANES] * piece[k : k + 1, :]
    row = as_row(jnp.sum(total, 1, keepdims=True))
    lane = lax.broadcasted_iota(jnp.int32, (1, LANES), 1)
    for e, extra in enumerate(extra_pieces):
        row = row + jnp.where(lane == kept + e, total_sum(extra * piece), 0.0)
    return row + jnp.where(lane == LANES - 1, total_sum(piece * piece), 0.0)


def inner_products(pieces, rows, basis, extras, riders, copies, after=()):
    listed = pieces if isinstance(pieces, (list, tuple)) else [pieces]
    stacked = listed is not pieces
    further = listed[0].shape[-2] - rows
    lines = 1 + further + sum(rider.shape[0] for rider in riders)

    def kernel(*refs):
        sources, (basis_ref,), extra_refs, rider_refs, _, (piece_ref, sent_ref) = take(
            refs, len(listed), 1, len(extras), len(riders), len(after)
        )
        if stacked:
            summed = jnp.sum(sources[0][...], 0)
        else:
            summed = sources[0][...]
            for source in sources[1:]:
                summed = summed + source[...]
        piece = summed[:rows]
        piece_ref[...] = piece
        sent = [basis_products(piece, basis_ref, [ref[...] for ref in extra_refs])]
        for ref in rider_refs:
            sent += [ref[k : k + 1, :] for k in range(ref.shape[0])]
        sent += [summed[rows + k : rows + k + 1] for k in range(further)]
        for at, line in enumerate(sent):
            shape = (copies, 1, LANES)
            sent_ref[:, :, at * LANES : (at + 1) * LANES] = jnp.broadcast_to(line[None], shape)

    return call(
        kernel,
        [(rows, LANES), (copies, 1, lines * LANES)],
        [*listed, basis, *extras, *riders, *after],
    )


def received_row(received_ref, at):
    lines = received_ref[:, 0, at * LANES : (at + 1) * LANES]
    return jnp.sum(lines, 0, keepdims=True)


def received_gram(received_ref, first, packed_ref, peers):
    share = packed_ref.shape[0] // peers
    devices = received_ref.shape[0]
    lines = received_ref.shape[2] // LANES - first
    if lines < share:
        for k in range(lines):
            at = slice((first + k) * LANES, (first + k + 1) * LANES)
            for device in range(devices):
                i, peer = divmod(device, peers)
                to = peer * share + i * lines + k
                packed_ref[to : to + 1, :] = received_ref[device, :, at]
        return
    for k in range(share):
        at = slice((first + k) * LANES, (first + k + 1) * LANES)
        added = received_ref[0:peers, 0, at]
        for i in range(1, devices // peers):
            added = added + received_ref[i * peers : (i + 1) * peers, 0, at]
        for peer in range(peers):
            packed_ref[peer * share + k : peer * share + k + 1, :] = added[peer : peer + 1]


def first_vector(mine, received, piece, basis, right_packed, total, peers):
    kept = basis.shape[0]
    rows = piece.shape[0]
    padded = kept + GROUP
    share = right_packed.shape[0] // peers

    def kernel(mine_ref, received_ref, piece_ref, basis_ref, right_ref, *refs):
        messages, (unit_ref, gram_ref, scale_ref, packed_ref) = take(refs, peers)
        received_gram(received_ref, 1, packed_ref, peers)
        products = unpacked_gram(packed_ref[...], padded)
        sums = received_row(received_ref, 0) * (1.0 / total)
        combined, remaining, squared, scale = coefficients(sums, products, kept)
        inverse = 1.0 / scale
        for k, line in unit_lines(piece_ref[...], combined, basis_ref, [], inverse):
            unit_ref[pl.ds(k, 1), :] = line
            for message in messages:
                message[pl.ds(k, 1), :] = line
        for x, message in enumerate(messages):
            peer = jnp.bitwise_xor(mine_ref[0], x)
            message[rows:, :] = right_ref[pl.ds(peer * share, share), :]
        gram_ref[...] = wider_gram(products, kept, remaining, squared, inverse)
        scale_ref[...] = jnp.broadcast_to(scale, scale_ref.shape)

    outs = [(rows + share, LANES)] * peers + [(rows, LANES), (padded, LANES), (1, LANES)]
    return call(
        kernel,
        outs,
        [mine, received, piece, basis, right_packed],
        [SMEM] + [VMEM] * 4,
        [pltpu.VMEM(right_packed.shape, jnp.float32)],
    )


def new_vector(received, gram, piece, basis, extras, total, copies, peers, widen):
    kept = basis.shape[0]
    rows = piece.shape[0]
    size = kept + len(extras)
    padded = kept + GROUP
    grams = [] if gram is None else [gram]

    def kernel(received_ref, piece_ref, basis_ref, *refs):
        gram_refs, extra_refs, rest = take(refs, len(grams), len(extras))
        copies_refs, (unit_ref, scale_ref), wider_refs, scratch = take(
            rest, 1 if copies else 0, 2, 1 if widen else 0
        )
        if gram_refs:
            products = gram_refs[0][...]
        else:
            received_gram(received_ref, 2, scratch[0], peers)
            products = unpacked_gram(scratch[0][...], padded)
            lane_at = lax.broadcasted_iota(jnp.int32, (padded, LANES), 1)
            sub_at = lax.broadcasted_iota(jnp.int32, (padded, LANES), 0)
            row = received_row(received_ref, 1) * (1.0 / total)
            row = jnp.broadcast_to(row, (padded, LANES))
            column = jnp.sum(jnp.where(lane_at == sub_at, row, 0.0), 1, keepdims=True)
            products = jnp.where((lane_at == kept) & (sub_at <= kept), column, products)
            products = jnp.where((sub_at == kept) & (lane_at <= kept), row, products)
        sums = received_row(received_ref, 0) * (1.0 / total)
        combined, remaining, squared, scale = coefficients(sums, products, size)
        inverse = 1.0 / scale
        extra_pieces = [ref[...] for ref in extra_refs]
        for k, line in unit_lines(piece_ref[...], combined, basis_ref, extra_pieces, inverse):
            unit_ref[pl.ds(k, 1), :] = line
            for ref in copies_refs:
                for copy in range(copies):
                    ref[copy, pl.ds(k, 1), :] = line
        for ref in wider_refs:
            ref[...] = wider_gram(products, size, remaining, squared, inverse)
        scale_ref[...] = jnp.broadcast_to(scale, scale_ref.shape)

    outs = [(copies, rows, LANES)] if copies else []
    outs += [(rows, LANES), (1, LANES)] + ([(padded, LANES)] if widen else [])
    scratch = [] if grams else [pltpu.VMEM((kept // 2, LANES), jnp.float32)]
    return call(kernel, outs, [received, piece, basis, *grams, *extras], None, scratch)


def coefficients(sums, products, size):
    lane = lax.broadcasted_iota(jnp.int32, (1, LANES), 1)
    coeffs = jnp.where(lane < size, sums, 0.0)
    squares = jnp.sum(jnp.where(lane == LANES - 1, sums, 0.0), 1, keepdims=True)
    eye = diagonal(products.shape[0])
    coeffs_col = jnp.sum(jnp.where(eye, coeffs, 0.0), 1, keepdims=True)
    combined = 2.0 * coeffs_col - jnp.sum(products * coeffs, 1, keepdims=True)
    gram_comb = jnp.sum(products * as_row(combined), 1, keepdims=True)
    squared = squares + jnp.sum(combined * (gram_comb - 2.0 * coeffs_col), 0, keepdims=True)
    squared = jnp.maximum(squared, 0.0)
    return combined, coeffs_col - gram_comb, squared, jnp.sqrt(squared + EPSILON)


def unit_lines(piece, combined, basis_ref, extra_pieces, inverse):
    kept = basis_ref.shape[0]
    spread = jnp.broadcast_to(combined[:kept], (kept, LANES))
    for e, extra in enumerate(extra_pieces):
        piece = piece - combined[kept + e : kept + e + 1] * extra
    for k in range(piece.shape[0]):
        part = jnp.sum(spread * basis_ref[:, k * LANES : (k + 1) * LANES], 0, keepdims=True)
        yield k, (piece[k : k + 1, :] - part) * inverse


def wider_gram(products, size, remaining, squared, inverse):
    shape = products.shape
    remaining = remaining * inverse
    sub_at = lax.broadcasted_iota(jnp.int32, shape, 0)
    lane_at = lax.broadcasted_iota(jnp.int32, shape, 1)
    wider = jnp.where((lane_at == size) & (sub_at < size), remaining, products)
    wider = jnp.where((sub_at == size) & (lane_at < size), as_row(remaining), wider)
    return jnp.where((sub_at == size) & (lane_at == size), squared * inverse * inverse, wider)


def last_vector(received, gram, piece, basis, extras, total, lefts, rights, scales):
    kept = basis.shape[0]
    rows = piece.shape[0]
    left_rows = lefts[0].shape[0]
    size = kept + len(extras)
    steps = len(lefts)

    def kernel(received_ref, gram_ref, piece_ref, basis_ref, *refs):
        extra_refs, left_refs, right_refs, scale_refs, outs = take(
            refs, len(extras), len(lefts), len(rights), len(scales)
        )
        left_out, right_out, scales_out = outs
        sums = received_row(received_ref, 0) * (1.0 / total)
        combined, _, _, scale = coefficients(sums, gram_ref[...], size)
        extra_pieces = [ref[...] for ref in extra_refs]
        for k, line in unit_lines(piece_ref[...], combined, basis_ref, extra_pieces, 1.0 / scale):
            right_out[steps - 1, :, k * LANES : (k + 1) * LANES] = line
        for step, ref in enumerate(right_refs):
            for k in range(rows):
                right_out[step, :, k * LANES : (k + 1) * LANES] = ref[k : k + 1, :]
        for step, ref in enumerate(left_refs):
            for k in range(left_rows):
                left_out[step : step + 1, k * LANES : (k + 1) * LANES] = ref[k : k + 1, :]
        values = [ref[:, 0:1] for ref in scale_refs] + [scale]
        sub_at = lax.broadcasted_iota(jnp.int32, (2, steps), 0)
        lane_at = lax.broadcasted_iota(jnp.int32, (2, steps), 1)
        table = jnp.zeros((2, steps), jnp.float32)
        for at, value in enumerate(values):
            table = jnp.where((sub_at == at % 2) & (lane_at == at // 2), value, table)
        scales_out[...] = table

    outs = [(steps, left_rows * LANES), (steps, 1, rows * LANES), (2, steps)]
    return call(kernel, outs, [received, gram, piece, basis, *extras, *lefts, *rights, *scales])


def shards(tiles, tile_index, u_basis, v_basis, v_start):
    blocks = tiles[0]
    slots = tile_index[0]
    width = blocks.shape[1]
    cols_len = v_start.shape[0]
    col_blocks = cols_len // width
    row_count = lax.axis_size("row")
    col_count = lax.axis_size("col")
    devices = row_count * col_count
    left_piece = u_basis.shape[1]
    right_piece = v_basis.shape[2]
    rows_len = left_piece * col_count
    row_blocks = rows_len // width
    left_rows = left_piece // width
    right_rows = right_piece // width
    total_left = rows_len * row_count
    total_right = cols_len * col_count
    mine = lax.axis_index("col").reshape(1)
    mine_row = lax.axis_index("row").reshape(1)
    far_first = list(range(col_count - 1, 0, -1))

    whole_start = v_start.reshape(col_blocks, width)
    messages = start(mine, blocks, slots, whole_start, u_basis, row_blocks, total_left, col_count)
    right_basis, start_share, start_row, right_packed = right_start(
        mine_row, v_basis, whole_start, messages[0], total_right
    )
    arrived = exchange(messages, far_first, "col")

    lefts, rights, scales = ([], [], [])
    right_extras = [start_share]
    left_gram = right_gram = None
    for iteration in range(ITERS):
        last = iteration + 1 == ITERS
        after = [right_packed] if iteration == 0 else []
        piece, sent = inner_products(arrived, left_rows, u_basis, lefts, [], devices, after)
        summed_rows = swap(sent, BOTH)
        if iteration == 0:
            *messages, left_unit, left_gram, alpha = first_vector(
                mine, summed_rows, piece, u_basis, right_packed, total_left, col_count
            )
        else:
            left_unit, alpha, *wider = new_vector(
                summed_rows, left_gram, piece, u_basis, lefts, total_left, 0, col_count, not last
            )
            left_gram = wider[0] if wider else None
            messages = [left_unit] * col_count
        lefts = lefts + [left_unit]
        scales = scales + [alpha]
        hops = far_first if iteration == 0 else far_first[::-1]
        arrived = exchange(messages, hops, "col")
        chunks, *further = backward_product(
            mine, blocks, slots, arrived, hops, left_rows, col_blocks, row_count
        )
        received = swap(chunks, "row")
        riders = [start_row, *further] if iteration == 0 else []
        piece, sent = inner_products(received, right_rows, right_basis, right_extras, riders, devices)
        summed_rows = swap(sent, BOTH)
        if not last:
            copies, right_unit, beta, right_gram = new_vector(
                summed_rows,
                right_gram,
                piece,
                right_basis,
                right_extras,
                total_right,
                row_count,
                col_count,
                True,
            )
            rights = rights + [right_unit]
            right_extras = right_extras + [right_unit]
            scales = scales + [beta]
            joined = swap(copies, "row").reshape(col_blocks, width)
            messages = forward_messages(mine, blocks, slots, joined, row_blocks, col_count)
            arrived = exchange(messages, far_first, "col")
    return last_vector(
        summed_rows, right_gram, piece, right_basis, right_extras, total_right, lefts, rights, scales
    )


def solution(mesh):
    placed = (
        P("row", "col", None, None),
        P("row", "col"),
        P(None, ("row", "col")),
        P(None, "col", "row"),
        P("col"),
    )
    return jax.shard_map(
        shards,
        mesh=mesh,
        in_specs=placed,
        out_specs=(P(None, ("row", "col")), P(None, "col", "row"), P()),
        check_vma=False,
    )
```

```python
import jax
import jax.numpy as jnp
from jax import lax
from jax.experimental import pallas as pl
from jax.experimental.pallas import tpu as pltpu
from jax.sharding import PartitionSpec as P

ITERS = 2


HIGHEST = lax.Precision.HIGHEST
EPSILON = 1e-06
BOTH = ("row", "col")
LANES = 128
GROUP = 8
PARAMS = pltpu.CompilerParams(vmem_limit_bytes=8 * 2**20)
WIDE = pltpu.CompilerParams(vmem_limit_bytes=63950 * 2**10)
VMEM = pl.BlockSpec(memory_space=pltpu.VMEM)
HBM = pl.BlockSpec(memory_space=pltpu.HBM)


def swap(chunks, axis):
    return lax.all_to_all(chunks, axis, 0, 0, tiled=True)


def call(kernel, outs, args, specs=None, scratch=(), params=PARAMS):
    shapes = tuple(jax.ShapeDtypeStruct(shape, jnp.float32) for shape in outs)
    return pl.pallas_call(
        kernel,
        out_shape=shapes,
        in_specs=specs or [VMEM] * len(args),
        out_specs=tuple([VMEM] * len(outs)),
        scratch_shapes=list(scratch),
        compiler_params=params,
    )(*args)


def take(refs, *counts):
    refs = list(refs)
    groups = []
    for count in counts:
        groups.append(refs[:count])
        refs = refs[count:]
    return groups + [refs]


def exchange(messages, hops, axis):
    count = lax.axis_size(axis)
    arrived = [messages[0]]
    for x in hops:
        arrived.append(lax.ppermute(messages[x], axis, [(i, i ^ x) for i in range(count)]))
    return arrived


def three_parts(x, axis):
    high = x.astype(jnp.bfloat16)
    rest = x - high.astype(jnp.float32)
    middle = rest.astype(jnp.bfloat16)
    low = (rest - middle.astype(jnp.float32)).astype(jnp.bfloat16)
    return jnp.concatenate([high, middle, low], axis)


def diagonal(rows):
    shape = (rows, LANES)
    return lax.broadcasted_iota(jnp.int32, shape, 0) == lax.broadcasted_iota(jnp.int32, shape, 1)


def as_row(column):
    return jnp.sum(jnp.where(diagonal(column.shape[0]), column, 0.0), 0, keepdims=True)


def total_sum(x):
    return jnp.sum(jnp.sum(x, 0, keepdims=True), 1, keepdims=True)


def tile_sums(slots, tiles_ref, vector, product_ref, out_blocks, is_forward):
    count, width = tiles_ref.shape[0], tiles_ref.shape[1]
    in_blocks = vector.shape[0]
    divisor = in_blocks if is_forward else out_blocks
    row_blocks = out_blocks if is_forward else in_blocks
    slots = slots.astype(jnp.float32)
    at = lax.broadcasted_iota(jnp.int32, (count, count), 0)
    to = lax.broadcasted_iota(jnp.int32, (count, count), 1)
    slots = jnp.sum(jnp.where(at == to, slots, 0.0), 1, keepdims=True)
    starts = lax.broadcasted_iota(jnp.int32, (count, row_blocks), 1) * divisor
    passed = jnp.where(slots >= starts.astype(jnp.float32), 1.0, 0.0)
    row = jnp.sum(passed, 1, keepdims=True) - 1.0
    column = slots - row * divisor
    live = slots < row_blocks * divisor

    def hot(place, blocks):
        lane = lax.broadcasted_iota(jnp.int32, (count, blocks), 1).astype(jnp.float32)
        return jnp.where((lane == place) & live, 1.0, 0.0).astype(jnp.bfloat16)

    source = hot(column if is_forward else row, in_blocks)
    target = hot(row if is_forward else column, out_blocks)
    picked = jnp.dot(source, three_parts(vector, 1), preferred_element_type=jnp.float32)
    parts = [picked[:, k * width : (k + 1) * width] for k in range(3)]
    parts = jnp.concatenate(parts, 0).astype(jnp.bfloat16)
    contract = (((1,), (1,)), ((), ())) if is_forward else (((1,), (0,)), ((), ()))
    for t in range(count):
        result = lax.dot_general(parts, tiles_ref[t], contract, preferred_element_type=jnp.float32)
        product_ref[pl.ds(t, 1), :] = (
            result[t : t + 1]
            + result[count + t : count + t + 1]
            + result[2 * count + t : 2 * count + t + 1]
        )
    placed = lax.dot_general(
        target,
        three_parts(product_ref[...], 1),
        (((0,), (0,)), ((), ())),
        preferred_element_type=jnp.float32,
    )
    return placed[:, :width] + placed[:, width : 2 * width] + placed[:, 2 * width :]


def packed_gram(basis, total):
    gram = lax.dot_general(
        basis,
        basis,
        (((1,), (1,)), ((), ())),
        precision=HIGHEST,
        preferred_element_type=jnp.float32,
    )
    half = gram.shape[0] // 2
    return gram[:half] * (1.0 / total), gram[half:] * (1.0 / total)


def unpacked_gram(packed, padded):
    half = packed.shape[0]
    grams = jnp.concatenate(
        [
            packed,
            pltpu.roll(packed, LANES // 2, 1),
            jnp.zeros((padded - 2 * half, LANES), jnp.float32),
        ],
        0,
    )
    lane_at = lax.broadcasted_iota(jnp.int32, grams.shape, 1)
    return jnp.where(lane_at < 2 * half, grams, 0.0)


def start(tiles, slots, vector, basis, row_blocks, total, peers):
    count, width = tiles.shape[0], tiles.shape[1]
    kept = basis.shape[0]
    rows = row_blocks // peers
    share = kept * kept // LANES // peers

    def kernel(slots_hbm, tiles_hbm, vector_hbm, basis_hbm, *refs):
        outs, scratch = take(refs, peers)
        slots_ref, tiles_ref, vector_ref, basis_ref, dense_ref, packed_ref, product_ref, sems = scratch
        moves = [
            pltpu.make_async_copy(source, target, sems.at[at])
            for at, (source, target) in enumerate(
                (
                    (slots_hbm, slots_ref),
                    (vector_hbm, vector_ref),
                    (tiles_hbm, tiles_ref),
                    (basis_hbm, basis_ref),
                )
            )
        ]
        for move in moves:
            move.start()
        for move in moves[:3]:
            move.wait()
        dense_ref[...] = tile_sums(
            slots_ref[...], tiles_ref, vector_ref[...], product_ref, row_blocks, True
        )
        moves[3].wait()
        upper, lower = packed_gram(basis_ref[...], total)
        packed_ref[:, :kept] = upper
        packed_ref[:, kept:] = lower
        for x, out in enumerate(outs):
            peer = jnp.bitwise_xor(lax.axis_index("col"), x)
            out[:rows, :] = dense_ref[pl.ds(peer * rows, rows), :]
            out[rows:, :] = packed_ref[pl.ds(peer * share, share), :]

    scratch = [
        pltpu.VMEM(slots.shape, slots.dtype),
        pltpu.VMEM(tiles.shape, tiles.dtype),
        pltpu.VMEM(vector.shape, jnp.float32),
        pltpu.VMEM(basis.shape, jnp.float32),
        pltpu.VMEM((row_blocks, width), jnp.float32),
        pltpu.VMEM((kept // 2, 2 * kept), jnp.float32),
        pltpu.VMEM((count, width), jnp.float32),
        pltpu.SemaphoreType.DMA((4,)),
    ]
    return call(
        kernel,
        [(rows + share, width)] * peers,
        [slots, tiles, vector, basis],
        [HBM] * 4,
        scratch,
        WIDE,
    )


def right_start(v_basis, vector, after, total):
    kept, _, length = v_basis.shape
    rows = length // LANES

    def kernel(basis_ref, vector_ref, after_ref, flat_ref, piece_ref, row_ref, packed_ref):
        for k in range(rows):
            at = slice(k * LANES, (k + 1) * LANES)
            flat_ref[:, at] = basis_ref[:, 0, at]
        piece = vector_ref[pl.ds(lax.axis_index("row") * rows, rows), :]
        piece_ref[...] = piece
        row_ref[...] = basis_products(piece, flat_ref, [piece])
        upper, lower = packed_gram(flat_ref[...], total)
        packed_ref[:, :kept] = upper
        packed_ref[:, kept:] = lower

    return call(
        kernel,
        [(kept, length), (rows, LANES), (1, LANES), (kept // 2, 2 * kept)],
        [v_basis, vector, after],
    )


def forward_messages(tiles, slots, vector, row_blocks, peers):
    count, width = tiles.shape[0], tiles.shape[1]
    rows = row_blocks // peers

    def kernel(slots_ref, tiles_ref, vector_ref, *refs):
        outs, (dense_ref, product_ref) = take(refs, peers)
        dense_ref[...] = tile_sums(
            slots_ref[...], tiles_ref, vector_ref[...], product_ref, row_blocks, True
        )
        for x, out in enumerate(outs):
            peer = jnp.bitwise_xor(lax.axis_index("col"), x)
            out[...] = dense_ref[pl.ds(peer * rows, rows), :]

    scratch = [pltpu.VMEM((row_blocks, width), jnp.float32)]
    scratch += [pltpu.VMEM((count, width), jnp.float32)]
    return call(
        kernel,
        [(rows, width)] * peers,
        [slots, tiles, vector],
        None,
        scratch,
    )


def backward_product(tiles, slots, messages, hops, rows, col_blocks, peers_row):
    count, width = tiles.shape[0], tiles.shape[1]
    peers = len(messages)
    share = messages[0].shape[0] - rows
    chunk = col_blocks // peers_row
    joined = share // peers_row if share % peers_row == 0 else 0
    apart = share and not joined

    def kernel(slots_ref, tiles_ref, *refs):
        sources, rest = take(refs, peers)
        (chunks_ref,), apart_refs, scratch = take(rest, 1, 1 if apart else 0)
        vector_ref, product_ref = scratch
        for at, source in enumerate(sources):
            peer = jnp.bitwise_xor(lax.axis_index("col"), ([0] + hops)[at])
            vector_ref[pl.ds(peer * rows, rows), :] = source[:rows, :]
        dense = tile_sums(
            slots_ref[...], tiles_ref, vector_ref[...], product_ref, col_blocks, False
        )
        for i in range(peers_row):
            chunks_ref[i, :chunk, :] = dense[i * chunk : (i + 1) * chunk, :]
        if share:
            added = sources[0][rows:, :]
            for source in sources[1:]:
                added = added + source[rows:, :]
            for ref in apart_refs:
                ref[...] = added
            if joined:
                for i in range(peers_row):
                    chunks_ref[i, chunk:, :] = added[i * joined : (i + 1) * joined]

    scratch = [pltpu.VMEM((rows * peers, width), jnp.float32)]
    scratch += [pltpu.VMEM((count, width), jnp.float32)]
    outs = [(peers_row, chunk + joined, width)] + ([(share, width)] if apart else [])
    return call(
        kernel,
        outs,
        [slots, tiles, *messages],
        None,
        scratch,
    )


def basis_products(piece, basis_ref, extra_pieces):
    kept = basis_ref.shape[0]
    total = jnp.zeros((kept, LANES), jnp.float32)
    for k in range(piece.shape[0]):
        total = total + basis_ref[:, k * LANES : (k + 1) * LANES] * piece[k : k + 1, :]
    row = as_row(jnp.sum(total, 1, keepdims=True))
    lane = lax.broadcasted_iota(jnp.int32, (1, LANES), 1)
    for e, extra in enumerate(extra_pieces):
        row = row + jnp.where(lane == kept + e, total_sum(extra * piece), 0.0)
    return row + jnp.where(lane == LANES - 1, total_sum(piece * piece), 0.0)


def inner_products(pieces, rows, basis, extras, riders, copies, after=()):
    listed = pieces if isinstance(pieces, (list, tuple)) else [pieces]
    stacked = listed is not pieces
    further = listed[0].shape[-2] - rows
    lines = 1 + further + sum(rider.shape[0] for rider in riders)

    def kernel(*refs):
        sources, (basis_ref,), extra_refs, rider_refs, _, (piece_ref, sent_ref) = take(
            refs, len(listed), 1, len(extras), len(riders), len(after)
        )
        if stacked:
            summed = jnp.sum(sources[0][...], 0)
        else:
            summed = sources[0][...]
            for source in sources[1:]:
                summed = summed + source[...]
        piece = summed[:rows]
        piece_ref[...] = piece
        sent = [basis_products(piece, basis_ref, [ref[...] for ref in extra_refs])]
        for ref in rider_refs:
            sent += [ref[k : k + 1, :] for k in range(ref.shape[0])]
        sent += [summed[rows + k : rows + k + 1] for k in range(further)]
        for at, line in enumerate(sent):
            shape = (copies, 1, LANES)
            sent_ref[:, :, at * LANES : (at + 1) * LANES] = jnp.broadcast_to(line[None], shape)

    return call(
        kernel,
        [(rows, LANES), (copies, 1, lines * LANES)],
        [*listed, basis, *extras, *riders, *after],
    )


def received_row(received_ref, at):
    lines = received_ref[:, 0, at * LANES : (at + 1) * LANES]
    return jnp.sum(lines, 0, keepdims=True)


def received_gram(received_ref, first, packed_ref, peers):
    share = packed_ref.shape[0] // peers
    devices = received_ref.shape[0]
    lines = received_ref.shape[2] // LANES - first
    if lines < share:
        for k in range(lines):
            at = slice((first + k) * LANES, (first + k + 1) * LANES)
            for device in range(devices):
                i, peer = divmod(device, peers)
                to = peer * share + i * lines + k
                packed_ref[to : to + 1, :] = received_ref[device, :, at]
        return
    for k in range(share):
        at = slice((first + k) * LANES, (first + k + 1) * LANES)
        added = received_ref[0:peers, 0, at]
        for i in range(1, devices // peers):
            added = added + received_ref[i * peers : (i + 1) * peers, 0, at]
        for peer in range(peers):
            packed_ref[peer * share + k : peer * share + k + 1, :] = added[peer : peer + 1]


def first_vector(received, piece, basis, right_packed, total, peers):
    kept = basis.shape[0]
    rows = piece.shape[0]
    padded = kept + GROUP
    share = right_packed.shape[0] // peers

    def kernel(received_ref, piece_ref, basis_ref, right_ref, *refs):
        messages, (unit_ref, gram_ref, scale_ref, packed_ref) = take(refs, peers)
        received_gram(received_ref, 1, packed_ref, peers)
        products = unpacked_gram(packed_ref[...], padded)
        sums = received_row(received_ref, 0) * (1.0 / total)
        combined, remaining, squared, scale = coefficients(sums, products, kept)
        inverse = 1.0 / scale
        for k, line in unit_lines(piece_ref[...], combined, basis_ref, [], inverse):
            unit_ref[pl.ds(k, 1), :] = line
            for message in messages:
                message[pl.ds(k, 1), :] = line
        for x, message in enumerate(messages):
            peer = jnp.bitwise_xor(lax.axis_index("col"), x)
            message[rows:, :] = right_ref[pl.ds(peer * share, share), :]
        gram_ref[...] = wider_gram(products, kept, remaining, squared, inverse)
        scale_ref[...] = jnp.broadcast_to(scale, scale_ref.shape)

    outs = [(rows + share, LANES)] * peers + [(rows, LANES), (padded, LANES), (1, LANES)]
    return call(
        kernel,
        outs,
        [received, piece, basis, right_packed],
        None,
        [pltpu.VMEM(right_packed.shape, jnp.float32)],
    )


def new_vector(received, gram, piece, basis, extras, total, copies, peers, widen):
    kept = basis.shape[0]
    rows = piece.shape[0]
    size = kept + len(extras)
    padded = kept + GROUP
    grams = [] if gram is None else [gram]

    def kernel(received_ref, piece_ref, basis_ref, *refs):
        gram_refs, extra_refs, rest = take(refs, len(grams), len(extras))
        copies_refs, (unit_ref, scale_ref), wider_refs, scratch = take(
            rest, 1 if copies else 0, 2, 1 if widen else 0
        )
        if gram_refs:
            products = gram_refs[0][...]
        else:
            received_gram(received_ref, 2, scratch[0], peers)
            products = unpacked_gram(scratch[0][...], padded)
            lane_at = lax.broadcasted_iota(jnp.int32, (padded, LANES), 1)
            sub_at = lax.broadcasted_iota(jnp.int32, (padded, LANES), 0)
            row = received_row(received_ref, 1) * (1.0 / total)
            row = jnp.broadcast_to(row, (padded, LANES))
            column = jnp.sum(jnp.where(lane_at == sub_at, row, 0.0), 1, keepdims=True)
            products = jnp.where((lane_at == kept) & (sub_at <= kept), column, products)
            products = jnp.where((sub_at == kept) & (lane_at <= kept), row, products)
        sums = received_row(received_ref, 0) * (1.0 / total)
        combined, remaining, squared, scale = coefficients(sums, products, size)
        inverse = 1.0 / scale
        extra_pieces = [ref[...] for ref in extra_refs]
        for k, line in unit_lines(piece_ref[...], combined, basis_ref, extra_pieces, inverse):
            unit_ref[pl.ds(k, 1), :] = line
            for ref in copies_refs:
                for copy in range(copies):
                    ref[copy, pl.ds(k, 1), :] = line
        for ref in wider_refs:
            ref[...] = wider_gram(products, size, remaining, squared, inverse)
        scale_ref[...] = jnp.broadcast_to(scale, scale_ref.shape)

    outs = [(copies, rows, LANES)] if copies else []
    outs += [(rows, LANES), (1, LANES)] + ([(padded, LANES)] if widen else [])
    scratch = [] if grams else [pltpu.VMEM((kept // 2, LANES), jnp.float32)]
    return call(kernel, outs, [received, piece, basis, *grams, *extras], None, scratch)


def coefficients(sums, products, size):
    lane = lax.broadcasted_iota(jnp.int32, (1, LANES), 1)
    coeffs = jnp.where(lane < size, sums, 0.0)
    squares = jnp.sum(jnp.where(lane == LANES - 1, sums, 0.0), 1, keepdims=True)
    eye = diagonal(products.shape[0])
    coeffs_col = jnp.sum(jnp.where(eye, coeffs, 0.0), 1, keepdims=True)
    combined = 2.0 * coeffs_col - jnp.sum(products * coeffs, 1, keepdims=True)
    gram_comb = jnp.sum(products * as_row(combined), 1, keepdims=True)
    squared = squares + jnp.sum(combined * (gram_comb - 2.0 * coeffs_col), 0, keepdims=True)
    squared = jnp.maximum(squared, 0.0)
    return combined, coeffs_col - gram_comb, squared, jnp.sqrt(squared + EPSILON)


def unit_lines(piece, combined, basis_ref, extra_pieces, inverse):
    kept = basis_ref.shape[0]
    spread = jnp.broadcast_to(combined[:kept], (kept, LANES))
    for e, extra in enumerate(extra_pieces):
        piece = piece - combined[kept + e : kept + e + 1] * extra
    for k in range(piece.shape[0]):
        part = jnp.sum(spread * basis_ref[:, k * LANES : (k + 1) * LANES], 0, keepdims=True)
        yield k, (piece[k : k + 1, :] - part) * inverse


def wider_gram(products, size, remaining, squared, inverse):
    shape = products.shape
    remaining = remaining * inverse
    sub_at = lax.broadcasted_iota(jnp.int32, shape, 0)
    lane_at = lax.broadcasted_iota(jnp.int32, shape, 1)
    wider = jnp.where((lane_at == size) & (sub_at < size), remaining, products)
    wider = jnp.where((sub_at == size) & (lane_at < size), as_row(remaining), wider)
    return jnp.where((sub_at == size) & (lane_at == size), squared * inverse * inverse, wider)


def last_vector(received, gram, piece, basis, extras, total, lefts, rights, scales):
    kept = basis.shape[0]
    rows = piece.shape[0]
    left_rows = lefts[0].shape[0]
    size = kept + len(extras)
    steps = len(lefts)

    def kernel(received_ref, gram_ref, piece_ref, basis_ref, *refs):
        extra_refs, left_refs, right_refs, scale_refs, outs = take(
            refs, len(extras), len(lefts), len(rights), len(scales)
        )
        left_out, right_out, scales_out = outs
        sums = received_row(received_ref, 0) * (1.0 / total)
        combined, _, _, scale = coefficients(sums, gram_ref[...], size)
        extra_pieces = [ref[...] for ref in extra_refs]
        for k, line in unit_lines(piece_ref[...], combined, basis_ref, extra_pieces, 1.0 / scale):
            right_out[steps - 1, :, k * LANES : (k + 1) * LANES] = line
        for step, ref in enumerate(right_refs):
            for k in range(rows):
                right_out[step, :, k * LANES : (k + 1) * LANES] = ref[k : k + 1, :]
        for step, ref in enumerate(left_refs):
            for k in range(left_rows):
                left_out[step : step + 1, k * LANES : (k + 1) * LANES] = ref[k : k + 1, :]
        values = [ref[:, 0:1] for ref in scale_refs] + [scale]
        sub_at = lax.broadcasted_iota(jnp.int32, (2, steps), 0)
        lane_at = lax.broadcasted_iota(jnp.int32, (2, steps), 1)
        table = jnp.zeros((2, steps), jnp.float32)
        for at, value in enumerate(values):
            table = jnp.where((sub_at == at % 2) & (lane_at == at // 2), value, table)
        scales_out[...] = table

    outs = [(steps, left_rows * LANES), (steps, 1, rows * LANES), (2, steps)]
    return call(kernel, outs, [received, gram, piece, basis, *extras, *lefts, *rights, *scales])


def shards(tiles, tile_index, u_basis, v_basis, v_start):
    blocks = tiles[0]
    slots = tile_index
    width = blocks.shape[1]
    cols_len = v_start.shape[0]
    col_blocks = cols_len // width
    row_count = lax.axis_size("row")
    col_count = lax.axis_size("col")
    devices = row_count * col_count
    left_piece = u_basis.shape[1]
    right_piece = v_basis.shape[2]
    rows_len = left_piece * col_count
    row_blocks = rows_len // width
    left_rows = left_piece // width
    right_rows = right_piece // width
    total_left = rows_len * row_count
    total_right = cols_len * col_count
    hop_order = list(range(2, col_count)) + [1]

    whole_start = v_start.reshape(col_blocks, width)
    messages = start(blocks, slots, whole_start, u_basis, row_blocks, total_left, col_count)
    right_basis, start_share, start_row, right_packed = right_start(
        v_basis, whole_start, messages[0], total_right
    )
    arrived = exchange(messages, hop_order, "col")

    lefts, rights, scales = ([], [], [])
    right_extras = [start_share]
    left_gram = right_gram = None
    for iteration in range(ITERS):
        last = iteration + 1 == ITERS
        after = [right_packed] if iteration == 0 else []
        piece, sent = inner_products(arrived, left_rows, u_basis, lefts, [], devices, after)
        summed_rows = swap(sent, BOTH)
        if iteration == 0:
            *messages, left_unit, left_gram, alpha = first_vector(
                summed_rows, piece, u_basis, right_packed, total_left, col_count
            )
        else:
            left_unit, alpha, *wider = new_vector(
                summed_rows, left_gram, piece, u_basis, lefts, total_left, 0, col_count, not last
            )
            left_gram = wider[0] if wider else None
            messages = [left_unit] * col_count
        lefts = lefts + [left_unit]
        scales = scales + [alpha]
        hops = hop_order if iteration == 0 else hop_order[::-1]
        arrived = exchange(messages, hops, "col")
        chunks, *further = backward_product(
            blocks, slots, arrived, hops, left_rows, col_blocks, row_count
        )
        received = swap(chunks, "row")
        riders = [start_row, *further] if iteration == 0 else []
        piece, sent = inner_products(received, right_rows, right_basis, right_extras, riders, devices)
        summed_rows = swap(sent, BOTH)
        if not last:
            copies, right_unit, beta, right_gram = new_vector(
                summed_rows,
                right_gram,
                piece,
                right_basis,
                right_extras,
                total_right,
                row_count,
                col_count,
                True,
            )
            rights = rights + [right_unit]
            right_extras = right_extras + [right_unit]
            scales = scales + [beta]
            joined = swap(copies, "row").reshape(col_blocks, width)
            messages = forward_messages(blocks, slots, joined, row_blocks, col_count)
            arrived = exchange(messages, hop_order, "col")
    return last_vector(
        summed_rows, right_gram, piece, right_basis, right_extras, total_right, lefts, rights, scales
    )


def solution(mesh):
    placed = (
        P("row", "col", None, None),
        P("row", "col"),
        P(None, ("row", "col")),
        P(None, "col", "row"),
        P("col"),
    )
    return jax.shard_map(
        shards,
        mesh=mesh,
        in_specs=placed,
        out_specs=(P(None, ("row", "col")), P(None, "col", "row"), P()),
        check_vma=False,
    )
```

```python
import jax
import jax.numpy as jnp
from jax import lax
from jax.experimental import pallas as pl
from jax.experimental.pallas import tpu as pltpu
from jax.sharding import PartitionSpec as P

ITERS = 2


HIGHEST = lax.Precision.HIGHEST
EPSILON = 1e-06
BOTH = ("row", "col")
LANES = 128
GROUP = 8
PARAMS = pltpu.CompilerParams(vmem_limit_bytes=8 * 2**20)
WIDE = pltpu.CompilerParams(vmem_limit_bytes=63950 * 2**10)
VMEM = pl.BlockSpec(memory_space=pltpu.VMEM)
HBM = pl.BlockSpec(memory_space=pltpu.HBM)


def swap(chunks, axis):
    return lax.all_to_all(chunks, axis, 0, 0, tiled=True)


def call(kernel, outs, args, specs=None, scratch=(), params=PARAMS):
    shapes = tuple(jax.ShapeDtypeStruct(shape, jnp.float32) for shape in outs)
    return pl.pallas_call(
        kernel,
        out_shape=shapes,
        in_specs=specs or [VMEM] * len(args),
        out_specs=tuple([VMEM] * len(outs)),
        scratch_shapes=list(scratch),
        compiler_params=params,
    )(*args)


def take(refs, *counts):
    refs = list(refs)
    groups = []
    for count in counts:
        groups.append(refs[:count])
        refs = refs[count:]
    return groups + [refs]


def exchange(messages, hops, axis):
    count = lax.axis_size(axis)
    arrived = [messages[0]]
    for x in hops:
        arrived.append(lax.ppermute(messages[x], axis, [(i, i ^ x) for i in range(count)]))
    return arrived


def three_parts(x, axis):
    high = x.astype(jnp.bfloat16)
    rest = x - high.astype(jnp.float32)
    middle = rest.astype(jnp.bfloat16)
    low = (rest - middle.astype(jnp.float32)).astype(jnp.bfloat16)
    return jnp.concatenate([high, middle, low], axis)


def diagonal(rows):
    shape = (rows, LANES)
    return lax.broadcasted_iota(jnp.int32, shape, 0) == lax.broadcasted_iota(jnp.int32, shape, 1)


def as_row(column):
    return jnp.sum(jnp.where(diagonal(column.shape[0]), column, 0.0), 0, keepdims=True)


def total_sum(x):
    return jnp.sum(jnp.sum(x, 0, keepdims=True), 1, keepdims=True)


def tile_sums(slots, tiles_ref, vector, out_blocks, is_forward):
    count, width = tiles_ref.shape[0], tiles_ref.shape[1]
    in_blocks = vector.shape[0]
    divisor = in_blocks if is_forward else out_blocks
    row_blocks = out_blocks if is_forward else in_blocks
    slots = slots.astype(jnp.float32)
    at = lax.broadcasted_iota(jnp.int32, (count, count), 0)
    to = lax.broadcasted_iota(jnp.int32, (count, count), 1)
    slots = jnp.sum(jnp.where(at == to, slots, 0.0), 1, keepdims=True)
    starts = lax.broadcasted_iota(jnp.int32, (count, row_blocks), 1) * divisor
    passed = jnp.where(slots >= starts.astype(jnp.float32), 1.0, 0.0)
    row = jnp.sum(passed, 1, keepdims=True) - 1.0
    column = slots - row * divisor
    live = slots < row_blocks * divisor

    def hot(place, blocks):
        lane = lax.broadcasted_iota(jnp.int32, (count, blocks), 1).astype(jnp.float32)
        return jnp.where((lane == place) & live, 1.0, 0.0).astype(jnp.bfloat16)

    source = hot(column if is_forward else row, in_blocks)
    target = hot(row if is_forward else column, out_blocks)
    picked = jnp.dot(source, three_parts(vector, 1), preferred_element_type=jnp.float32)
    own = lax.broadcasted_iota(jnp.int32, (count, width), 0)
    spread = []
    for k in range(3):
        part = picked[:, k * width : (k + 1) * width]
        blocks = [jnp.where(own == t, part, 0.0) for t in range(count)]
        spread.append(jnp.concatenate(blocks, 1))
    spread = jnp.concatenate(spread, 0).astype(jnp.bfloat16)
    if is_forward:
        flat = jnp.concatenate([tiles_ref[t] for t in range(count)], 1)
        contract = (((1,), (1,)), ((), ()))
    else:
        flat = tiles_ref[...].reshape(count * width, width)
        contract = (((1,), (0,)), ((), ()))
    result = lax.dot_general(spread, flat, contract, preferred_element_type=jnp.float32)
    product = result[:count] + result[count : 2 * count] + result[2 * count :]
    placed = lax.dot_general(
        target,
        three_parts(product, 1),
        (((0,), (0,)), ((), ())),
        preferred_element_type=jnp.float32,
    )
    return placed[:, :width] + placed[:, width : 2 * width] + placed[:, 2 * width :]


def packed_gram(basis, total):
    kept = basis.shape[0]
    contract = (((1,), (1,)), ((), ()))
    parts = three_parts(basis, 0)
    high = lax.dot_general(
        parts, parts[:kept], contract, preferred_element_type=jnp.float32
    )
    middle = lax.dot_general(
        parts[kept : 2 * kept], parts[kept : 2 * kept], contract, preferred_element_type=jnp.float32
    )
    cross = high[kept : 2 * kept] + high[2 * kept :]
    gram = high[:kept] + middle + cross + jnp.transpose(cross)
    half = kept // 2
    return gram[:half] * (1.0 / total), gram[half:] * (1.0 / total)


def unpacked_gram(packed, padded):
    half = packed.shape[0]
    grams = jnp.concatenate(
        [
            packed,
            pltpu.roll(packed, LANES // 2, 1),
            jnp.zeros((padded - 2 * half, LANES), jnp.float32),
        ],
        0,
    )
    lane_at = lax.broadcasted_iota(jnp.int32, grams.shape, 1)
    return jnp.where(lane_at < 2 * half, grams, 0.0)


def start(tiles, slots, vector, basis, row_blocks, total, peers):
    count, width = tiles.shape[0], tiles.shape[1]
    kept = basis.shape[0]
    rows = row_blocks // peers
    share = kept * kept // LANES // peers

    def kernel(slots_hbm, tiles_hbm, vector_hbm, basis_hbm, *refs):
        outs, scratch = take(refs, peers)
        slots_ref, tiles_ref, vector_ref, basis_ref, dense_ref, packed_ref, sems = scratch
        moves = [
            pltpu.make_async_copy(source, target, sems.at[at])
            for at, (source, target) in enumerate(
                (
                    (slots_hbm, slots_ref),
                    (vector_hbm, vector_ref),
                    (tiles_hbm, tiles_ref),
                    (basis_hbm, basis_ref),
                )
            )
        ]
        for move in moves:
            move.start()
        for move in moves[:3]:
            move.wait()
        dense_ref[...] = tile_sums(
            slots_ref[...], tiles_ref, vector_ref[...], row_blocks, True
        )
        moves[3].wait()
        upper, lower = packed_gram(basis_ref[...], total)
        packed_ref[:, :kept] = upper
        packed_ref[:, kept:] = lower
        for x, out in enumerate(outs):
            peer = jnp.bitwise_xor(lax.axis_index("col"), x)
            out[:rows, :] = dense_ref[pl.ds(peer * rows, rows), :]
            out[rows:, :] = packed_ref[pl.ds(peer * share, share), :]

    scratch = [
        pltpu.VMEM(slots.shape, slots.dtype),
        pltpu.VMEM(tiles.shape, tiles.dtype),
        pltpu.VMEM(vector.shape, jnp.float32),
        pltpu.VMEM(basis.shape, jnp.float32),
        pltpu.VMEM((row_blocks, width), jnp.float32),
        pltpu.VMEM((kept // 2, 2 * kept), jnp.float32),
        pltpu.SemaphoreType.DMA((4,)),
    ]
    return call(
        kernel,
        [(rows + share, width)] * peers,
        [slots, tiles, vector, basis],
        [HBM] * 4,
        scratch,
        WIDE,
    )


def right_start(v_basis, vector, after, total):
    kept, _, length = v_basis.shape
    rows = length // LANES

    def kernel(basis_ref, vector_ref, after_ref, flat_ref, piece_ref, row_ref, packed_ref):
        for k in range(rows):
            at = slice(k * LANES, (k + 1) * LANES)
            flat_ref[:, at] = basis_ref[:, 0, at]
        piece = vector_ref[pl.ds(lax.axis_index("row") * rows, rows), :]
        piece_ref[...] = piece
        row_ref[...] = basis_products(piece, flat_ref, [piece])
        upper, lower = packed_gram(flat_ref[...], total)
        packed_ref[:, :kept] = upper
        packed_ref[:, kept:] = lower

    return call(
        kernel,
        [(kept, length), (rows, LANES), (1, LANES), (kept // 2, 2 * kept)],
        [v_basis, vector, after],
    )


def forward_messages(tiles, slots, vector, row_blocks, peers):
    count, width = tiles.shape[0], tiles.shape[1]
    rows = row_blocks // peers

    def kernel(slots_ref, tiles_ref, vector_ref, *refs):
        outs, (dense_ref,) = take(refs, peers)
        dense_ref[...] = tile_sums(
            slots_ref[...], tiles_ref, vector_ref[...], row_blocks, True
        )
        for x, out in enumerate(outs):
            peer = jnp.bitwise_xor(lax.axis_index("col"), x)
            out[...] = dense_ref[pl.ds(peer * rows, rows), :]

    scratch = [pltpu.VMEM((row_blocks, width), jnp.float32)]
    return call(
        kernel,
        [(rows, width)] * peers,
        [slots, tiles, vector],
        None,
        scratch,
    )


def backward_product(tiles, slots, messages, hops, rows, col_blocks, peers_row):
    count, width = tiles.shape[0], tiles.shape[1]
    peers = len(messages)
    share = messages[0].shape[0] - rows
    chunk = col_blocks // peers_row
    joined = share // peers_row if share % peers_row == 0 else 0
    apart = share and not joined

    def kernel(slots_ref, tiles_ref, *refs):
        sources, rest = take(refs, peers)
        (chunks_ref,), apart_refs, scratch = take(rest, 1, 1 if apart else 0)
        (vector_ref,) = scratch
        for at, source in enumerate(sources):
            peer = jnp.bitwise_xor(lax.axis_index("col"), ([0] + hops)[at])
            vector_ref[pl.ds(peer * rows, rows), :] = source[:rows, :]
        dense = tile_sums(
            slots_ref[...], tiles_ref, vector_ref[...], col_blocks, False
        )
        for i in range(peers_row):
            chunks_ref[i, :chunk, :] = dense[i * chunk : (i + 1) * chunk, :]
        if share:
            added = sources[0][rows:, :]
            for source in sources[1:]:
                added = added + source[rows:, :]
            for ref in apart_refs:
                ref[...] = added
            if joined:
                for i in range(peers_row):
                    chunks_ref[i, chunk:, :] = added[i * joined : (i + 1) * joined]

    scratch = [pltpu.VMEM((rows * peers, width), jnp.float32)]
    outs = [(peers_row, chunk + joined, width)] + ([(share, width)] if apart else [])
    return call(
        kernel,
        outs,
        [slots, tiles, *messages],
        None,
        scratch,
    )


def basis_products(piece, basis_ref, extra_pieces):
    kept = basis_ref.shape[0]
    total = jnp.zeros((kept, LANES), jnp.float32)
    for k in range(piece.shape[0]):
        total = total + basis_ref[:, k * LANES : (k + 1) * LANES] * piece[k : k + 1, :]
    row = as_row(jnp.sum(total, 1, keepdims=True))
    lane = lax.broadcasted_iota(jnp.int32, (1, LANES), 1)
    for e, extra in enumerate(extra_pieces):
        row = row + jnp.where(lane == kept + e, total_sum(extra * piece), 0.0)
    return row + jnp.where(lane == LANES - 1, total_sum(piece * piece), 0.0)


def inner_products(pieces, rows, basis, extras, riders, copies, after=()):
    listed = pieces if isinstance(pieces, (list, tuple)) else [pieces]
    stacked = listed is not pieces
    further = listed[0].shape[-2] - rows
    lines = 1 + further + sum(rider.shape[0] for rider in riders)

    def kernel(*refs):
        sources, (basis_ref,), extra_refs, rider_refs, _, (piece_ref, sent_ref) = take(
            refs, len(listed), 1, len(extras), len(riders), len(after)
        )
        if stacked:
            summed = jnp.sum(sources[0][...], 0)
        else:
            summed = sources[0][...]
            for source in sources[1:]:
                summed = summed + source[...]
        piece = summed[:rows]
        piece_ref[...] = piece
        sent = [basis_products(piece, basis_ref, [ref[...] for ref in extra_refs])]
        for ref in rider_refs:
            sent += [ref[k : k + 1, :] for k in range(ref.shape[0])]
        sent += [summed[rows + k : rows + k + 1] for k in range(further)]
        for at, line in enumerate(sent):
            shape = (copies, 1, LANES)
            sent_ref[:, :, at * LANES : (at + 1) * LANES] = jnp.broadcast_to(line[None], shape)

    return call(
        kernel,
        [(rows, LANES), (copies, 1, lines * LANES)],
        [*listed, basis, *extras, *riders, *after],
    )


def received_row(received_ref, at):
    lines = received_ref[:, 0, at * LANES : (at + 1) * LANES]
    return jnp.sum(lines, 0, keepdims=True)


def received_gram(received_ref, first, packed_ref, peers):
    share = packed_ref.shape[0] // peers
    devices = received_ref.shape[0]
    lines = received_ref.shape[2] // LANES - first
    if lines < share:
        for k in range(lines):
            at = slice((first + k) * LANES, (first + k + 1) * LANES)
            for device in range(devices):
                i, peer = divmod(device, peers)
                to = peer * share + i * lines + k
                packed_ref[to : to + 1, :] = received_ref[device, :, at]
        return
    for k in range(share):
        at = slice((first + k) * LANES, (first + k + 1) * LANES)
        added = received_ref[0:peers, 0, at]
        for i in range(1, devices // peers):
            added = added + received_ref[i * peers : (i + 1) * peers, 0, at]
        for peer in range(peers):
            packed_ref[peer * share + k : peer * share + k + 1, :] = added[peer : peer + 1]


def first_vector(received, piece, basis, right_packed, total, peers):
    kept = basis.shape[0]
    rows = piece.shape[0]
    padded = kept + GROUP
    share = right_packed.shape[0] // peers

    def kernel(received_ref, piece_ref, basis_ref, right_ref, *refs):
        messages, (unit_ref, gram_ref, scale_ref, packed_ref) = take(refs, peers)
        received_gram(received_ref, 1, packed_ref, peers)
        products = unpacked_gram(packed_ref[...], padded)
        sums = received_row(received_ref, 0) * (1.0 / total)
        combined, remaining, squared, scale = coefficients(sums, products, kept)
        inverse = 1.0 / scale
        for k, line in unit_lines(piece_ref[...], combined, basis_ref, [], inverse):
            unit_ref[pl.ds(k, 1), :] = line
            for message in messages:
                message[pl.ds(k, 1), :] = line
        for x, message in enumerate(messages):
            peer = jnp.bitwise_xor(lax.axis_index("col"), x)
            message[rows:, :] = right_ref[pl.ds(peer * share, share), :]
        gram_ref[...] = wider_gram(products, kept, remaining, squared, inverse)
        scale_ref[...] = jnp.broadcast_to(scale, scale_ref.shape)

    outs = [(rows + share, LANES)] * peers + [(rows, LANES), (padded, LANES), (1, LANES)]
    return call(
        kernel,
        outs,
        [received, piece, basis, right_packed],
        None,
        [pltpu.VMEM(right_packed.shape, jnp.float32)],
    )


def new_vector(received, gram, piece, basis, extras, total, copies, peers, widen):
    kept = basis.shape[0]
    rows = piece.shape[0]
    size = kept + len(extras)
    padded = kept + GROUP
    grams = [] if gram is None else [gram]

    def kernel(received_ref, piece_ref, basis_ref, *refs):
        gram_refs, extra_refs, rest = take(refs, len(grams), len(extras))
        copies_refs, (unit_ref, scale_ref), wider_refs, scratch = take(
            rest, 1 if copies else 0, 2, 1 if widen else 0
        )
        if gram_refs:
            products = gram_refs[0][...]
        else:
            received_gram(received_ref, 2, scratch[0], peers)
            products = unpacked_gram(scratch[0][...], padded)
            lane_at = lax.broadcasted_iota(jnp.int32, (padded, LANES), 1)
            sub_at = lax.broadcasted_iota(jnp.int32, (padded, LANES), 0)
            row = received_row(received_ref, 1) * (1.0 / total)
            row = jnp.broadcast_to(row, (padded, LANES))
            column = jnp.sum(jnp.where(lane_at == sub_at, row, 0.0), 1, keepdims=True)
            products = jnp.where((lane_at == kept) & (sub_at <= kept), column, products)
            products = jnp.where((sub_at == kept) & (lane_at <= kept), row, products)
        sums = received_row(received_ref, 0) * (1.0 / total)
        combined, remaining, squared, scale = coefficients(sums, products, size)
        inverse = 1.0 / scale
        extra_pieces = [ref[...] for ref in extra_refs]
        for k, line in unit_lines(piece_ref[...], combined, basis_ref, extra_pieces, inverse):
            unit_ref[pl.ds(k, 1), :] = line
            for ref in copies_refs:
                for copy in range(copies):
                    ref[copy, pl.ds(k, 1), :] = line
        for ref in wider_refs:
            ref[...] = wider_gram(products, size, remaining, squared, inverse)
        scale_ref[...] = jnp.broadcast_to(scale, scale_ref.shape)

    outs = [(copies, rows, LANES)] if copies else []
    outs += [(rows, LANES), (1, LANES)] + ([(padded, LANES)] if widen else [])
    scratch = [] if grams else [pltpu.VMEM((kept // 2, LANES), jnp.float32)]
    return call(kernel, outs, [received, piece, basis, *grams, *extras], None, scratch)


def coefficients(sums, products, size):
    lane = lax.broadcasted_iota(jnp.int32, (1, LANES), 1)
    coeffs = jnp.where(lane < size, sums, 0.0)
    squares = jnp.sum(jnp.where(lane == LANES - 1, sums, 0.0), 1, keepdims=True)
    eye = diagonal(products.shape[0])
    coeffs_col = jnp.sum(jnp.where(eye, coeffs, 0.0), 1, keepdims=True)
    combined = 2.0 * coeffs_col - jnp.sum(products * coeffs, 1, keepdims=True)
    gram_comb = jnp.sum(products * as_row(combined), 1, keepdims=True)
    squared = squares + jnp.sum(combined * (gram_comb - 2.0 * coeffs_col), 0, keepdims=True)
    squared = jnp.maximum(squared, 0.0)
    return combined, coeffs_col - gram_comb, squared, jnp.sqrt(squared + EPSILON)


def unit_lines(piece, combined, basis_ref, extra_pieces, inverse):
    kept = basis_ref.shape[0]
    spread = jnp.broadcast_to(combined[:kept], (kept, LANES))
    for e, extra in enumerate(extra_pieces):
        piece = piece - combined[kept + e : kept + e + 1] * extra
    for k in range(piece.shape[0]):
        part = jnp.sum(spread * basis_ref[:, k * LANES : (k + 1) * LANES], 0, keepdims=True)
        yield k, (piece[k : k + 1, :] - part) * inverse


def wider_gram(products, size, remaining, squared, inverse):
    shape = products.shape
    remaining = remaining * inverse
    sub_at = lax.broadcasted_iota(jnp.int32, shape, 0)
    lane_at = lax.broadcasted_iota(jnp.int32, shape, 1)
    wider = jnp.where((lane_at == size) & (sub_at < size), remaining, products)
    wider = jnp.where((sub_at == size) & (lane_at < size), as_row(remaining), wider)
    return jnp.where((sub_at == size) & (lane_at == size), squared * inverse * inverse, wider)


def last_vector(received, gram, piece, basis, extras, total, lefts, rights, scales):
    kept = basis.shape[0]
    rows = piece.shape[0]
    left_rows = lefts[0].shape[0]
    size = kept + len(extras)
    steps = len(lefts)

    def kernel(received_ref, gram_ref, piece_ref, basis_ref, *refs):
        extra_refs, left_refs, right_refs, scale_refs, outs = take(
            refs, len(extras), len(lefts), len(rights), len(scales)
        )
        left_out, right_out, scales_out = outs
        sums = received_row(received_ref, 0) * (1.0 / total)
        combined, _, _, scale = coefficients(sums, gram_ref[...], size)
        extra_pieces = [ref[...] for ref in extra_refs]
        for k, line in unit_lines(piece_ref[...], combined, basis_ref, extra_pieces, 1.0 / scale):
            right_out[steps - 1, :, k * LANES : (k + 1) * LANES] = line
        for step, ref in enumerate(right_refs):
            for k in range(rows):
                right_out[step, :, k * LANES : (k + 1) * LANES] = ref[k : k + 1, :]
        for step, ref in enumerate(left_refs):
            for k in range(left_rows):
                left_out[step : step + 1, k * LANES : (k + 1) * LANES] = ref[k : k + 1, :]
        values = [ref[:, 0:1] for ref in scale_refs] + [scale]
        sub_at = lax.broadcasted_iota(jnp.int32, (2, steps), 0)
        lane_at = lax.broadcasted_iota(jnp.int32, (2, steps), 1)
        table = jnp.zeros((2, steps), jnp.float32)
        for at, value in enumerate(values):
            table = jnp.where((sub_at == at % 2) & (lane_at == at // 2), value, table)
        scales_out[...] = table

    outs = [(steps, left_rows * LANES), (steps, 1, rows * LANES), (2, steps)]
    return call(kernel, outs, [received, gram, piece, basis, *extras, *lefts, *rights, *scales])


def shards(tiles, tile_index, u_basis, v_basis, v_start):
    blocks = tiles[0]
    slots = tile_index
    width = blocks.shape[1]
    cols_len = v_start.shape[0]
    col_blocks = cols_len // width
    row_count = lax.axis_size("row")
    col_count = lax.axis_size("col")
    devices = row_count * col_count
    left_piece = u_basis.shape[1]
    right_piece = v_basis.shape[2]
    rows_len = left_piece * col_count
    row_blocks = rows_len // width
    left_rows = left_piece // width
    right_rows = right_piece // width
    total_left = rows_len * row_count
    total_right = cols_len * col_count
    hop_order = list(range(2, col_count)) + [1]

    whole_start = v_start.reshape(col_blocks, width)
    messages = start(blocks, slots, whole_start, u_basis, row_blocks, total_left, col_count)
    right_basis, start_share, start_row, right_packed = right_start(
        v_basis, whole_start, messages[0], total_right
    )
    arrived = exchange(messages, hop_order, "col")

    lefts, rights, scales = ([], [], [])
    right_extras = [start_share]
    left_gram = right_gram = None
    for iteration in range(ITERS):
        last = iteration + 1 == ITERS
        after = [right_packed] if iteration == 0 else []
        piece, sent = inner_products(arrived, left_rows, u_basis, lefts, [], devices, after)
        summed_rows = swap(sent, BOTH)
        if iteration == 0:
            *messages, left_unit, left_gram, alpha = first_vector(
                summed_rows, piece, u_basis, right_packed, total_left, col_count
            )
        else:
            left_unit, alpha, *wider = new_vector(
                summed_rows, left_gram, piece, u_basis, lefts, total_left, 0, col_count, not last
            )
            left_gram = wider[0] if wider else None
            messages = [left_unit] * col_count
        lefts = lefts + [left_unit]
        scales = scales + [alpha]
        hops = hop_order if iteration == 0 else hop_order[::-1]
        arrived = exchange(messages, hops, "col")
        chunks, *further = backward_product(
            blocks, slots, arrived, hops, left_rows, col_blocks, row_count
        )
        received = swap(chunks, "row")
        riders = [start_row, *further] if iteration == 0 else []
        piece, sent = inner_products(received, right_rows, right_basis, right_extras, riders, devices)
        summed_rows = swap(sent, BOTH)
        if not last:
            copies, right_unit, beta, right_gram = new_vector(
                summed_rows,
                right_gram,
                piece,
                right_basis,
                right_extras,
                total_right,
                row_count,
                col_count,
                True,
            )
            rights = rights + [right_unit]
            right_extras = right_extras + [right_unit]
            scales = scales + [beta]
            joined = swap(copies, "row").reshape(col_blocks, width)
            messages = forward_messages(blocks, slots, joined, row_blocks, col_count)
            arrived = exchange(messages, hop_order, "col")
    return last_vector(
        summed_rows, right_gram, piece, right_basis, right_extras, total_right, lefts, rights, scales
    )


def solution(mesh):
    placed = (
        P("row", "col", None, None),
        P("row", "col"),
        P(None, ("row", "col")),
        P(None, "col", "row"),
        P("col"),
    )
    return jax.shard_map(
        shards,
        mesh=mesh,
        in_specs=placed,
        out_specs=(P(None, ("row", "col")), P(None, "col", "row"), P()),
        check_vma=False,
    )
```

```python
import jax
import jax.numpy as jnp
from jax import lax
from jax.experimental import pallas as pl
from jax.experimental.pallas import tpu as pltpu
from jax.sharding import PartitionSpec as P

ITERS = 2


HIGHEST = lax.Precision.HIGHEST
EPSILON = 1e-06
BOTH = ("row", "col")
LANES = 128
GROUP = 8
PARAMS = pltpu.CompilerParams(vmem_limit_bytes=8 * 2**20)
WIDE = pltpu.CompilerParams(vmem_limit_bytes=63950 * 2**10)
VMEM = pl.BlockSpec(memory_space=pltpu.VMEM)
HBM = pl.BlockSpec(memory_space=pltpu.HBM)


def swap(chunks, axis):
    return lax.all_to_all(chunks, axis, 0, 0, tiled=True)


def call(kernel, outs, args, specs=None, scratch=(), params=PARAMS):
    shapes = tuple(jax.ShapeDtypeStruct(shape, jnp.float32) for shape in outs)
    return pl.pallas_call(
        kernel,
        out_shape=shapes,
        in_specs=specs or [VMEM] * len(args),
        out_specs=tuple([VMEM] * len(outs)),
        scratch_shapes=list(scratch),
        compiler_params=params,
    )(*args)


def take(refs, *counts):
    refs = list(refs)
    groups = []
    for count in counts:
        groups.append(refs[:count])
        refs = refs[count:]
    return groups + [refs]


def exchange(messages, hops, axis):
    count = lax.axis_size(axis)
    arrived = [messages[0]]
    for x in hops:
        arrived.append(lax.ppermute(messages[x], axis, [(i, i ^ x) for i in range(count)]))
    return arrived


def three_parts(x, axis):
    high = x.astype(jnp.bfloat16)
    rest = x - high.astype(jnp.float32)
    middle = rest.astype(jnp.bfloat16)
    low = (rest - middle.astype(jnp.float32)).astype(jnp.bfloat16)
    return jnp.concatenate([high, middle, low], axis)


def diagonal(rows):
    shape = (rows, LANES)
    return lax.broadcasted_iota(jnp.int32, shape, 0) == lax.broadcasted_iota(jnp.int32, shape, 1)


def as_row(column):
    return jnp.sum(jnp.where(diagonal(column.shape[0]), column, 0.0), 0, keepdims=True)


def total_sum(x):
    return jnp.sum(jnp.sum(x, 0, keepdims=True), 1, keepdims=True)


def tile_sums(slots, tiles_ref, vector, out_blocks, is_forward):
    count, width = tiles_ref.shape[0], tiles_ref.shape[1]
    in_blocks = vector.shape[0]
    divisor = in_blocks if is_forward else out_blocks
    row_blocks = out_blocks if is_forward else in_blocks
    slots = slots.astype(jnp.float32)
    at = lax.broadcasted_iota(jnp.int32, (count, count), 0)
    to = lax.broadcasted_iota(jnp.int32, (count, count), 1)
    slots = jnp.sum(jnp.where(at == to, slots, 0.0), 1, keepdims=True)
    starts = lax.broadcasted_iota(jnp.int32, (count, row_blocks), 1) * divisor
    passed = jnp.where(slots >= starts.astype(jnp.float32), 1.0, 0.0)
    row = jnp.sum(passed, 1, keepdims=True) - 1.0
    column = slots - row * divisor
    live = slots < row_blocks * divisor

    def hot(place, blocks):
        lane = lax.broadcasted_iota(jnp.int32, (count, blocks), 1).astype(jnp.float32)
        return jnp.where((lane == place) & live, 1.0, 0.0).astype(jnp.bfloat16)

    source = hot(column if is_forward else row, in_blocks)
    target = hot(row if is_forward else column, out_blocks)
    picked = jnp.dot(source, three_parts(vector, 1), preferred_element_type=jnp.float32)
    own = lax.broadcasted_iota(jnp.int32, (count, width), 0)
    spread = []
    for k in range(3):
        part = picked[:, k * width : (k + 1) * width]
        blocks = [jnp.where(own == t, part, 0.0) for t in range(count)]
        spread.append(jnp.concatenate(blocks, 1))
    spread = jnp.concatenate(spread, 0).astype(jnp.bfloat16)
    if is_forward:
        flat = jnp.concatenate([tiles_ref[t] for t in range(count)], 1)
        contract = (((1,), (1,)), ((), ()))
    else:
        flat = tiles_ref[...].reshape(count * width, width)
        contract = (((1,), (0,)), ((), ()))
    result = lax.dot_general(spread, flat, contract, preferred_element_type=jnp.float32)
    product = result[:count] + result[count : 2 * count] + result[2 * count :]
    placed = lax.dot_general(
        target,
        three_parts(product, 1),
        (((0,), (0,)), ((), ())),
        preferred_element_type=jnp.float32,
    )
    return placed[:, :width] + placed[:, width : 2 * width] + placed[:, 2 * width :]


def packed_gram(basis, total):
    kept = basis.shape[0]
    contract = (((1,), (1,)), ((), ()))
    parts = three_parts(basis, 0)
    high = lax.dot_general(
        parts, parts[:kept], contract, preferred_element_type=jnp.float32
    )
    middle = lax.dot_general(
        parts[kept : 2 * kept], parts[kept : 2 * kept], contract, preferred_element_type=jnp.float32
    )
    cross = high[kept : 2 * kept] + high[2 * kept :]
    gram = high[:kept] + middle + cross + jnp.transpose(cross)
    half = kept // 2
    return gram[:half] * (1.0 / total), gram[half:] * (1.0 / total)


def unpacked_gram(packed, padded):
    half = packed.shape[0]
    grams = jnp.concatenate(
        [
            packed,
            pltpu.roll(packed, LANES // 2, 1),
            jnp.zeros((padded - 2 * half, LANES), jnp.float32),
        ],
        0,
    )
    lane_at = lax.broadcasted_iota(jnp.int32, grams.shape, 1)
    return jnp.where(lane_at < 2 * half, grams, 0.0)


def start(tiles, slots, vector, basis, row_blocks, total, peers):
    count, width = tiles.shape[0], tiles.shape[1]
    kept = basis.shape[0]
    rows = row_blocks // peers
    share = kept * kept // LANES // peers

    def kernel(slots_hbm, tiles_hbm, vector_hbm, basis_hbm, *refs):
        outs, scratch = take(refs, peers)
        slots_ref, tiles_ref, vector_ref, basis_ref, dense_ref, packed_ref, sems = scratch
        moves = [
            pltpu.make_async_copy(source, target, sems.at[at])
            for at, (source, target) in enumerate(
                (
                    (slots_hbm, slots_ref),
                    (vector_hbm, vector_ref),
                    (tiles_hbm, tiles_ref),
                    (basis_hbm, basis_ref),
                )
            )
        ]
        for move in moves:
            move.start()
        for move in moves[:3]:
            move.wait()
        dense_ref[...] = tile_sums(
            slots_ref[...], tiles_ref, vector_ref[...], row_blocks, True
        )
        moves[3].wait()
        upper, lower = packed_gram(basis_ref[...], total)
        packed_ref[:, :kept] = upper
        packed_ref[:, kept:] = lower
        for x, out in enumerate(outs):
            peer = jnp.bitwise_xor(lax.axis_index("col"), x)
            out[:rows, :] = dense_ref[pl.ds(peer * rows, rows), :]
            out[rows:, :] = packed_ref[pl.ds(peer * share, share), :]

    scratch = [
        pltpu.VMEM(slots.shape, slots.dtype),
        pltpu.VMEM(tiles.shape, tiles.dtype),
        pltpu.VMEM(vector.shape, jnp.float32),
        pltpu.VMEM(basis.shape, jnp.float32),
        pltpu.VMEM((row_blocks, width), jnp.float32),
        pltpu.VMEM((kept // 2, 2 * kept), jnp.float32),
        pltpu.SemaphoreType.DMA((4,)),
    ]
    return call(
        kernel,
        [(rows + share, width)] * peers,
        [slots, tiles, vector, basis],
        [HBM] * 4,
        scratch,
        WIDE,
    )


def right_start(v_basis, vector, after, total):
    kept, _, length = v_basis.shape
    rows = length // LANES

    def kernel(basis_ref, vector_ref, after_ref, flat_ref, piece_ref, row_ref, packed_ref):
        for k in range(rows):
            at = slice(k * LANES, (k + 1) * LANES)
            flat_ref[:, at] = basis_ref[:, 0, at]
        piece = vector_ref[pl.ds(lax.axis_index("row") * rows, rows), :]
        piece_ref[...] = piece
        row_ref[...] = basis_products(piece, flat_ref, [piece])
        upper, lower = packed_gram(flat_ref[...], total)
        packed_ref[:, :kept] = upper
        packed_ref[:, kept:] = lower

    return call(
        kernel,
        [(kept, length), (rows, LANES), (1, LANES), (kept // 2, 2 * kept)],
        [v_basis, vector, after],
    )


def forward_messages(tiles, slots, vector, row_blocks, peers):
    count, width = tiles.shape[0], tiles.shape[1]
    rows = row_blocks // peers

    def kernel(slots_ref, tiles_ref, vector_ref, *refs):
        outs, (dense_ref,) = take(refs, peers)
        dense_ref[...] = tile_sums(
            slots_ref[...], tiles_ref, vector_ref[...], row_blocks, True
        )
        for x, out in enumerate(outs):
            peer = jnp.bitwise_xor(lax.axis_index("col"), x)
            out[...] = dense_ref[pl.ds(peer * rows, rows), :]

    scratch = [pltpu.VMEM((row_blocks, width), jnp.float32)]
    return call(
        kernel,
        [(rows, width)] * peers,
        [slots, tiles, vector],
        None,
        scratch,
    )


def backward_product(tiles, slots, messages, hops, rows, col_blocks, peers_row):
    count, width = tiles.shape[0], tiles.shape[1]
    peers = len(messages)
    share = messages[0].shape[0] - rows
    chunk = col_blocks // peers_row
    joined = share // peers_row if share % peers_row == 0 else 0
    apart = share and not joined

    def kernel(slots_ref, tiles_ref, *refs):
        sources, rest = take(refs, peers)
        (chunks_ref,), apart_refs, scratch = take(rest, 1, 1 if apart else 0)
        (vector_ref,) = scratch
        for at, source in enumerate(sources):
            peer = jnp.bitwise_xor(lax.axis_index("col"), ([0] + hops)[at])
            vector_ref[pl.ds(peer * rows, rows), :] = source[:rows, :]
        dense = tile_sums(
            slots_ref[...], tiles_ref, vector_ref[...], col_blocks, False
        )
        for i in range(peers_row):
            chunks_ref[i, :chunk, :] = dense[i * chunk : (i + 1) * chunk, :]
        if share:
            added = sources[0][rows:, :]
            for source in sources[1:]:
                added = added + source[rows:, :]
            for ref in apart_refs:
                ref[...] = added
            if joined:
                for i in range(peers_row):
                    chunks_ref[i, chunk:, :] = added[i * joined : (i + 1) * joined]

    scratch = [pltpu.VMEM((rows * peers, width), jnp.float32)]
    outs = [(peers_row, chunk + joined, width)] + ([(share, width)] if apart else [])
    return call(
        kernel,
        outs,
        [slots, tiles, *messages],
        None,
        scratch,
    )


def basis_products(piece, basis_ref, extra_pieces):
    kept = basis_ref.shape[0]
    total = jnp.zeros((kept, LANES), jnp.float32)
    for k in range(piece.shape[0]):
        total = total + basis_ref[:, k * LANES : (k + 1) * LANES] * piece[k : k + 1, :]
    row = as_row(jnp.sum(total, 1, keepdims=True))
    lane = lax.broadcasted_iota(jnp.int32, (1, LANES), 1)
    for e, extra in enumerate(extra_pieces):
        row = row + jnp.where(lane == kept + e, total_sum(extra * piece), 0.0)
    return row + jnp.where(lane == LANES - 1, total_sum(piece * piece), 0.0)


def inner_products(pieces, rows, basis, extras, riders, copies, after=()):
    listed = pieces if isinstance(pieces, (list, tuple)) else [pieces]
    stacked = listed is not pieces
    further = listed[0].shape[-2] - rows
    lines = 1 + further + sum(rider.shape[0] for rider in riders)

    def kernel(*refs):
        sources, (basis_ref,), extra_refs, rider_refs, _, (piece_ref, sent_ref) = take(
            refs, len(listed), 1, len(extras), len(riders), len(after)
        )
        if stacked:
            summed = jnp.sum(sources[0][...], 0)
        else:
            summed = sources[0][...]
            for source in sources[1:]:
                summed = summed + source[...]
        piece = summed[:rows]
        piece_ref[...] = piece
        sent = [basis_products(piece, basis_ref, [ref[...] for ref in extra_refs])]
        for ref in rider_refs:
            sent += [ref[k : k + 1, :] for k in range(ref.shape[0])]
        sent += [summed[rows + k : rows + k + 1] for k in range(further)]
        for at, line in enumerate(sent):
            shape = (copies, 1, LANES)
            sent_ref[:, :, at * LANES : (at + 1) * LANES] = jnp.broadcast_to(line[None], shape)

    return call(
        kernel,
        [(rows, LANES), (copies, 1, lines * LANES)],
        [*listed, basis, *extras, *riders, *after],
    )


def received_row(received_ref, at):
    lines = received_ref[:, 0, at * LANES : (at + 1) * LANES]
    return jnp.sum(lines, 0, keepdims=True)


def received_gram(received_ref, first, packed_ref, peers):
    share = packed_ref.shape[0] // peers
    devices = received_ref.shape[0]
    lines = received_ref.shape[2] // LANES - first
    if lines < share:
        for k in range(lines):
            at = slice((first + k) * LANES, (first + k + 1) * LANES)
            for device in range(devices):
                i, peer = divmod(device, peers)
                to = peer * share + i * lines + k
                packed_ref[to : to + 1, :] = received_ref[device, :, at]
        return
    for k in range(share):
        at = slice((first + k) * LANES, (first + k + 1) * LANES)
        group = max(peers, GROUP)
        lines_at = received_ref[:, 0, at]
        summed = lines_at[0:group]
        for i in range(1, devices // group):
            summed = summed + lines_at[i * group : (i + 1) * group]
        added = summed[0:peers]
        for i in range(1, group // peers):
            added = added + summed[i * peers : (i + 1) * peers]
        for peer in range(peers):
            packed_ref[peer * share + k : peer * share + k + 1, :] = added[peer : peer + 1]


def first_vector(received, piece, basis, right_packed, total, peers):
    kept = basis.shape[0]
    rows = piece.shape[0]
    padded = kept + GROUP
    share = right_packed.shape[0] // peers

    def kernel(received_ref, piece_ref, basis_ref, right_ref, *refs):
        messages, (unit_ref, gram_ref, scale_ref, packed_ref) = take(refs, peers)
        received_gram(received_ref, 1, packed_ref, peers)
        products = unpacked_gram(packed_ref[...], padded)
        sums = received_row(received_ref, 0) * (1.0 / total)
        combined, remaining, squared, scale = coefficients(sums, products, kept)
        inverse = 1.0 / scale
        for k, line in unit_lines(piece_ref[...], combined, basis_ref, [], inverse):
            unit_ref[pl.ds(k, 1), :] = line
            for message in messages:
                message[pl.ds(k, 1), :] = line
        for x, message in enumerate(messages):
            peer = jnp.bitwise_xor(lax.axis_index("col"), x)
            message[rows:, :] = right_ref[pl.ds(peer * share, share), :]
        gram_ref[...] = wider_gram(products, kept, remaining, squared, inverse)
        scale_ref[...] = jnp.broadcast_to(scale, scale_ref.shape)

    outs = [(rows + share, LANES)] * peers + [(rows, LANES), (padded, LANES), (1, LANES)]
    return call(
        kernel,
        outs,
        [received, piece, basis, right_packed],
        None,
        [pltpu.VMEM(right_packed.shape, jnp.float32)],
    )


def new_vector(received, gram, piece, basis, extras, total, copies, peers, widen):
    kept = basis.shape[0]
    rows = piece.shape[0]
    size = kept + len(extras)
    padded = kept + GROUP
    grams = [] if gram is None else [gram]

    def kernel(received_ref, piece_ref, basis_ref, *refs):
        gram_refs, extra_refs, rest = take(refs, len(grams), len(extras))
        copies_refs, (unit_ref, scale_ref), wider_refs, scratch = take(
            rest, 1 if copies else 0, 2, 1 if widen else 0
        )
        if gram_refs:
            products = gram_refs[0][...]
        else:
            received_gram(received_ref, 2, scratch[0], peers)
            products = unpacked_gram(scratch[0][...], padded)
            lane_at = lax.broadcasted_iota(jnp.int32, (padded, LANES), 1)
            sub_at = lax.broadcasted_iota(jnp.int32, (padded, LANES), 0)
            row = received_row(received_ref, 1) * (1.0 / total)
            row = jnp.broadcast_to(row, (padded, LANES))
            column = jnp.sum(jnp.where(lane_at == sub_at, row, 0.0), 1, keepdims=True)
            products = jnp.where((lane_at == kept) & (sub_at <= kept), column, products)
            products = jnp.where((sub_at == kept) & (lane_at <= kept), row, products)
        sums = received_row(received_ref, 0) * (1.0 / total)
        combined, remaining, squared, scale = coefficients(sums, products, size)
        inverse = 1.0 / scale
        extra_pieces = [ref[...] for ref in extra_refs]
        for k, line in unit_lines(piece_ref[...], combined, basis_ref, extra_pieces, inverse):
            unit_ref[pl.ds(k, 1), :] = line
            for ref in copies_refs:
                for copy in range(copies):
                    ref[copy, pl.ds(k, 1), :] = line
        for ref in wider_refs:
            ref[...] = wider_gram(products, size, remaining, squared, inverse)
        scale_ref[...] = jnp.broadcast_to(scale, scale_ref.shape)

    outs = [(copies, rows, LANES)] if copies else []
    outs += [(rows, LANES), (1, LANES)] + ([(padded, LANES)] if widen else [])
    scratch = [] if grams else [pltpu.VMEM((kept // 2, LANES), jnp.float32)]
    return call(kernel, outs, [received, piece, basis, *grams, *extras], None, scratch)


def coefficients(sums, products, size):
    lane = lax.broadcasted_iota(jnp.int32, (1, LANES), 1)
    coeffs = jnp.where(lane < size, sums, 0.0)
    squares = jnp.sum(jnp.where(lane == LANES - 1, sums, 0.0), 1, keepdims=True)
    eye = diagonal(products.shape[0])
    coeffs_col = jnp.sum(jnp.where(eye, coeffs, 0.0), 1, keepdims=True)
    combined = 2.0 * coeffs_col - jnp.sum(products * coeffs, 1, keepdims=True)
    gram_comb = jnp.sum(products * as_row(combined), 1, keepdims=True)
    squared = squares + jnp.sum(combined * (gram_comb - 2.0 * coeffs_col), 0, keepdims=True)
    squared = jnp.maximum(squared, 0.0)
    return combined, coeffs_col - gram_comb, squared, jnp.sqrt(squared + EPSILON)


def unit_lines(piece, combined, basis_ref, extra_pieces, inverse):
    kept = basis_ref.shape[0]
    spread = jnp.broadcast_to(combined[:kept], (kept, LANES))
    for e, extra in enumerate(extra_pieces):
        piece = piece - combined[kept + e : kept + e + 1] * extra
    for k in range(piece.shape[0]):
        part = jnp.sum(spread * basis_ref[:, k * LANES : (k + 1) * LANES], 0, keepdims=True)
        yield k, (piece[k : k + 1, :] - part) * inverse


def wider_gram(products, size, remaining, squared, inverse):
    shape = products.shape
    remaining = remaining * inverse
    sub_at = lax.broadcasted_iota(jnp.int32, shape, 0)
    lane_at = lax.broadcasted_iota(jnp.int32, shape, 1)
    wider = jnp.where((lane_at == size) & (sub_at < size), remaining, products)
    wider = jnp.where((sub_at == size) & (lane_at < size), as_row(remaining), wider)
    return jnp.where((sub_at == size) & (lane_at == size), squared * inverse * inverse, wider)


def last_vector(received, gram, piece, basis, extras, total, lefts, rights, scales):
    kept = basis.shape[0]
    rows = piece.shape[0]
    left_rows = lefts[0].shape[0]
    size = kept + len(extras)
    steps = len(lefts)

    def kernel(received_ref, gram_ref, piece_ref, basis_ref, *refs):
        extra_refs, left_refs, right_refs, scale_refs, outs = take(
            refs, len(extras), len(lefts), len(rights), len(scales)
        )
        left_out, right_out, scales_out = outs
        sums = received_row(received_ref, 0) * (1.0 / total)
        combined, _, _, scale = coefficients(sums, gram_ref[...], size)
        extra_pieces = [ref[...] for ref in extra_refs]
        for k, line in unit_lines(piece_ref[...], combined, basis_ref, extra_pieces, 1.0 / scale):
            right_out[steps - 1, :, k * LANES : (k + 1) * LANES] = line
        for step, ref in enumerate(right_refs):
            for k in range(rows):
                right_out[step, :, k * LANES : (k + 1) * LANES] = ref[k : k + 1, :]
        for step, ref in enumerate(left_refs):
            for k in range(left_rows):
                left_out[step : step + 1, k * LANES : (k + 1) * LANES] = ref[k : k + 1, :]
        values = [ref[:, 0:1] for ref in scale_refs] + [scale]
        sub_at = lax.broadcasted_iota(jnp.int32, (2, steps), 0)
        lane_at = lax.broadcasted_iota(jnp.int32, (2, steps), 1)
        table = jnp.zeros((2, steps), jnp.float32)
        for at, value in enumerate(values):
            table = jnp.where((sub_at == at % 2) & (lane_at == at // 2), value, table)
        scales_out[...] = table

    outs = [(steps, left_rows * LANES), (steps, 1, rows * LANES), (2, steps)]
    return call(kernel, outs, [received, gram, piece, basis, *extras, *lefts, *rights, *scales])


def shards(tiles, tile_index, u_basis, v_basis, v_start):
    blocks = tiles[0]
    slots = tile_index
    width = blocks.shape[1]
    cols_len = v_start.shape[0]
    col_blocks = cols_len // width
    row_count = lax.axis_size("row")
    col_count = lax.axis_size("col")
    devices = row_count * col_count
    left_piece = u_basis.shape[1]
    right_piece = v_basis.shape[2]
    rows_len = left_piece * col_count
    row_blocks = rows_len // width
    left_rows = left_piece // width
    right_rows = right_piece // width
    total_left = rows_len * row_count
    total_right = cols_len * col_count
    hop_order = list(range(2, col_count)) + [1]

    whole_start = v_start.reshape(col_blocks, width)
    messages = start(blocks, slots, whole_start, u_basis, row_blocks, total_left, col_count)
    right_basis, start_share, start_row, right_packed = right_start(
        v_basis, whole_start, messages[0], total_right
    )
    arrived = exchange(messages, hop_order, "col")

    lefts, rights, scales = ([], [], [])
    right_extras = [start_share]
    left_gram = right_gram = None
    for iteration in range(ITERS):
        last = iteration + 1 == ITERS
        after = [right_packed] if iteration == 0 else []
        piece, sent = inner_products(arrived, left_rows, u_basis, lefts, [], devices, after)
        summed_rows = swap(sent, BOTH)
        if iteration == 0:
            *messages, left_unit, left_gram, alpha = first_vector(
                summed_rows, piece, u_basis, right_packed, total_left, col_count
            )
        else:
            left_unit, alpha, *wider = new_vector(
                summed_rows, left_gram, piece, u_basis, lefts, total_left, 0, col_count, not last
            )
            left_gram = wider[0] if wider else None
            messages = [left_unit] * col_count
        lefts = lefts + [left_unit]
        scales = scales + [alpha]
        hops = hop_order if iteration == 0 else hop_order[::-1]
        arrived = exchange(messages, hops, "col")
        chunks, *further = backward_product(
            blocks, slots, arrived, hops, left_rows, col_blocks, row_count
        )
        received = swap(chunks, "row")
        riders = [start_row, *further] if iteration == 0 else []
        piece, sent = inner_products(received, right_rows, right_basis, right_extras, riders, devices)
        summed_rows = swap(sent, BOTH)
        if not last:
            copies, right_unit, beta, right_gram = new_vector(
                summed_rows,
                right_gram,
                piece,
                right_basis,
                right_extras,
                total_right,
                row_count,
                col_count,
                True,
            )
            rights = rights + [right_unit]
            right_extras = right_extras + [right_unit]
            scales = scales + [beta]
            joined = swap(copies, "row").reshape(col_blocks, width)
            messages = forward_messages(blocks, slots, joined, row_blocks, col_count)
            arrived = exchange(messages, hop_order, "col")
    return last_vector(
        summed_rows, right_gram, piece, right_basis, right_extras, total_right, lefts, rights, scales
    )


def solution(mesh):
    placed = (
        P("row", "col", None, None),
        P("row", "col"),
        P(None, ("row", "col")),
        P(None, "col", "row"),
        P("col"),
    )
    return jax.shard_map(
        shards,
        mesh=mesh,
        in_specs=placed,
        out_specs=(P(None, ("row", "col")), P(None, "col", "row"), P()),
        check_vma=False,
    )
```
